768 devices in a mesh: lon: 96 (over z, y), lat: 4 (over x_hi, core), rep: 2 (over x_lo).
Axes of the slice: x: 4 (x_hi: 2, x_lo: 2; x = x_hi * 2 + x_lo), y: 8, z: 12, core: 2. Of those that a mesh axis runs over, the one named last changes fastest.
Arguments:
- tokens: bfloat16 [2, 48, 1152, 192], P(None, ('lat', 'rep'), 'lon'), may hold values from -6 to 6
- cotangent: bfloat16 [2, 48, 1152, 192], P(None, ('lat', 'rep'), 'lon'), may hold values from -6 to 6
- region: int32 [2, 48, 1152], P(None, ('lat', 'rep'), 'lon'), may hold values from 0 to 2
- pos_index: int32 [144, 144], replicated, may hold values from 0 to 3311
- w_qkv: bfloat16 [192, 576], replicated, may hold values from -0.4375 to 0.4375
- w_proj: bfloat16 [192, 192], replicated, may hold values from -0.4375 to 0.4375
- bias_table: float32 [3312, 8, 6], P(None, ('lat', 'rep')), may hold values from -4 to 247
Outputs:
- grad_tokens: bfloat16 [2, 48, 1152, 192], P(None, ('lat', 'rep'), 'lon')
- grad_qkv: float32 [192, 576], replicated
- grad_proj: float32 [192, 192], replicated
- grad_bias: float32 [3312, 8, 6], P(None, ('lat', 'rep'))
The draws below stay inside these ranges and needn't reach their ends.
All inputs are finite; a program needn't handle non-finite values.
Results may differ from the reference program's by a relative error of at most 0.0096.
Values may be sent and summed in bfloat16 or wider, within the bound.
No kernel may reach another device: no remote copies, remote signals or barrier semaphores. Data moves between devices by JAX's collectives and lax.ppermute only.
A program may use at most 64 MiB of HBM per device.

```python
import jax
import jax.numpy as jnp
from jax import lax

C = 192
HEADS = 6
PL = 2
WIN = 144
BIAS_ROWS = 3312
LAT = 48
LON = 1152
TYPES = 8


def draw_bias_table(key, part):
    key_base = jax.random.fold_in(key, 0)
    table = jnp.clip(jax.random.normal(key_base, (BIAS_ROWS, TYPES, HEADS), jnp.float32), -4.0, 4.0)
    return table


def with_ends(entries, key, low, top_value):
    dims = entries.shape
    spot = [jax.random.randint(jax.random.fold_in(key, axis), (), 0, dims[axis]) for axis in range(len(dims))]
    entries = entries.at[tuple(spot)].set(low)
    longest = dims.index(max(dims))
    spot[longest] = (spot[longest] + 1) % dims[longest]
    return entries.at[tuple(spot)].set(top_value)


def steps_of(own_key, dims, cuts, least, largest):
    gain, own = 1.0, jax.random.fold_in(own_key, 6)
    for position, shards_of in cuts:
        draws = jnp.exp(jax.random.uniform(jax.random.fold_in(own, position), (shards_of,), jnp.float32, least / len(cuts), largest / len(cuts)))
        gain = gain * jnp.repeat(draws, dims[position] // shards_of).reshape([-1 if axis == position else 1 for axis in range(len(dims))])
    return gain


def gaussian(key, extent, deviation, reach, shards=(), kind=jnp.bfloat16):
    gain = steps_of(key, extent, shards, -0.22, 0.18) if shards else 1.0
    drawn = jax.random.normal(key, extent, jnp.float32) * deviation * gain
    return jnp.minimum(jnp.maximum(drawn, -reach), reach).astype(kind)


def setup_inputs(seed: int = 0) -> dict:
    keys = jax.random.split(jax.random.key(seed), 8)
    tokens = gaussian(keys[0], (PL, LAT, LON, C), 1.0, 6.0, ((1, 8), (2, 96)))
    cotangent = gaussian(keys[1], (PL, LAT, LON, C), 1.0, 6.0, ((1, 8), (2, 96)))
    region = with_ends(jax.random.randint(keys[2], (PL, LAT, LON), 0, 3), jax.random.fold_in(keys[2], 1), 0, 2).astype(jnp.int32)
    pos_index = with_ends(jax.random.randint(keys[3], (WIN, WIN), 0, BIAS_ROWS), jax.random.fold_in(keys[3], 1), 0, BIAS_ROWS - 1).astype(jnp.int32)
    w_qkv = gaussian(keys[4], (C, 3 * C), C ** -0.5, 0.4375)
    w_proj = gaussian(keys[5], (C, C), C ** -0.5, 0.4375)
    bias_table = draw_bias_table(jax.random.fold_in(keys[7], 71), 0)
    return {"tokens": tokens, "cotangent": cotangent, "region": region, "pos_index": pos_index, "w_qkv": w_qkv, "w_proj": w_proj, "bias_table": bias_table}


def contract(form, left, right):
    return jnp.einsum(form, left.astype(jnp.float32), right.astype(jnp.float32))

def window_grads(shifted, shifted_cot, region, pos_index, w_qkv, w_proj, bias_table):
    levels, lats, lons, width = shifted.shape
    pl_win, lat_win, lon_win = (levels // 2, lats // 6, lons // 12)
    heads = bias_table.shape[2]
    head_dim = width // heads
    scale = head_dim ** (-0.5)

    def windows_of(tensor):
        depth = tensor.shape[-1]
        tensor = tensor.reshape(pl_win, 2, lat_win, 6, lon_win, 12, depth)
        tensor = tensor.transpose(0, 2, 4, 1, 3, 5, 6)
        return tensor.reshape(pl_win, lat_win, lon_win, 144, depth)

    def tokens_of(tensor):
        depth = tensor.shape[-1]
        tensor = tensor.reshape(pl_win, lat_win, lon_win, 2, 6, 12, depth)
        tensor = tensor.transpose(0, 3, 1, 4, 2, 5, 6)
        return tensor.reshape(levels, lats, lons, depth)
    values = shifted.astype(jnp.float32)
    center = values - lax.optimization_barrier(jnp.mean(values, axis=-1, keepdims=True))
    inv_std = lax.rsqrt(lax.optimization_barrier(jnp.mean(center * center, axis=-1, keepdims=True)) + 1e-05)
    normed = center * inv_std
    hidden = windows_of(normed.astype(jnp.bfloat16))
    projected = contract('pabtc,cf->pabtf', hidden, w_qkv).astype(jnp.bfloat16)
    projected = projected.reshape(pl_win, lat_win, lon_win, 144, 3, heads, head_dim)
    query_rows = projected[:, :, :, :, 0]
    key_rows = projected[:, :, :, :, 1]
    value_rows = projected[:, :, :, :, 2]
    table_rows = bias_table[pos_index].reshape(144, 144, lat_win, pl_win, heads)
    table_rows = table_rows.transpose(3, 2, 4, 0, 1)[:, :, None]
    labels = windows_of(region[..., None])[..., 0]
    same = (labels[..., :, None] == labels[..., None, :])[:, :, :, None]
    scores = contract('pabqhd,pabkhd->pabhqk', query_rows, key_rows) * scale + table_rows
    scores = jnp.where(same, scores, -1000000000.0)
    top = lax.optimization_barrier(jnp.max(scores, axis=-1, keepdims=True))
    exponent = jnp.exp(scores - top)
    probability = exponent / lax.optimization_barrier(jnp.sum(exponent, axis=-1, keepdims=True))
    prob_half = probability.astype(jnp.bfloat16)
    attended = contract('pabhqk,pabkhd->pabqhd', prob_half, value_rows).astype(jnp.bfloat16)
    attended = attended.reshape(pl_win, lat_win, lon_win, 144, width)
    cot_win = windows_of(shifted_cot)
    grad_proj = contract('pabtc,pabtf->cf', attended, cot_win)
    grad_att = contract('pabtf,cf->pabtc', cot_win, w_proj).astype(jnp.bfloat16)
    grad_att = grad_att.reshape(pl_win, lat_win, lon_win, 144, heads, head_dim)
    grad_prob = contract('pabqhd,pabkhd->pabhqk', grad_att, value_rows)
    grad_value = contract('pabhqk,pabqhd->pabkhd', prob_half, grad_att)
    grad_scores = probability * (grad_prob - lax.optimization_barrier(jnp.sum(grad_prob * probability, axis=-1, keepdims=True)))
    folded = lax.optimization_barrier(jnp.sum(grad_scores, axis=2)).transpose(3, 4, 1, 0, 2).reshape(144 * 144, lat_win * pl_win * heads)
    grad_bias = jax.ops.segment_sum(folded, pos_index.reshape(-1), num_segments=bias_table.shape[0])
    grad_bias = grad_bias.reshape(bias_table.shape)
    scores_half = grad_scores.astype(jnp.bfloat16)
    grad_query = contract('pabhqk,pabkhd->pabqhd', scores_half, key_rows) * scale
    grad_key = contract('pabhqk,pabqhd->pabkhd', scores_half, query_rows) * scale
    grad_in = jnp.stack((grad_query, grad_key, grad_value), axis=4).astype(jnp.bfloat16)
    grad_in = grad_in.reshape(pl_win, lat_win, lon_win, 144, 3 * width)
    grad_qkv = contract('pabtc,pabtf->cf', hidden, grad_in)
    grad_hidden = tokens_of(contract('pabtf,cf->pabtc', grad_in, w_qkv))
    grad_norm = inv_std * (grad_hidden - lax.optimization_barrier(jnp.mean(grad_hidden, axis=-1, keepdims=True)) - normed * lax.optimization_barrier(jnp.mean(grad_hidden * normed, axis=-1, keepdims=True)))
    grad_shifted = shifted_cot.astype(jnp.float32) + grad_norm
    return (grad_shifted, grad_qkv, grad_proj, grad_bias)

def reference(tokens, cotangent, region, pos_index, w_qkv, w_proj, bias_table):
    shifted = jnp.roll(tokens, (-1, -3, -6), (0, 1, 2))
    shifted_cot = jnp.roll(cotangent, (-1, -3, -6), (0, 1, 2))
    columns = LON // 12
    width = tokens.shape[3]
    col_tok = shifted.reshape(PL, LAT, columns, 12, width).transpose(2, 0, 1, 3, 4)
    col_cot = shifted_cot.reshape(PL, LAT, columns, 12, width).transpose(2, 0, 1, 3, 4)
    col_reg = region.reshape(PL, LAT, columns, 12).transpose(2, 0, 1, 3)

    def column(carry, items):
        tok_col, cot_col, reg_col = items
        grad_col, grad_q, grad_p, grad_b = window_grads(tok_col, cot_col, reg_col, pos_index, w_qkv, w_proj, bias_table)
        return ((carry[0] + grad_q, carry[1] + grad_p, carry[2] + grad_b), grad_col)
    start = (jnp.zeros(w_qkv.shape, jnp.float32), jnp.zeros(w_proj.shape, jnp.float32), jnp.zeros(bias_table.shape, jnp.float32))
    totals, grad_cols = lax.scan(column, start, (col_tok, col_cot, col_reg))
    grad_shifted = grad_cols.transpose(1, 2, 0, 3, 4).reshape(PL, LAT, LON, width)
    grad_tokens = jnp.roll(grad_shifted, (1, 3, 6), (0, 1, 2)).astype(jnp.bfloat16)
    return (grad_tokens, totals[0], totals[1], totals[2])
```

```python
import functools

import jax
import jax.numpy as jnp
import numpy as np
from jax import lax
from jax.experimental import pallas as pl
from jax.experimental.pallas import tpu as pltpu
from jax.sharding import PartitionSpec as P

F32 = jnp.float32
BF16 = jnp.bfloat16
T = 144
C = 192
HEADS = 6
HD = 32
ROWS = 3312
BLKS = 26
PACK = 168
QUADS = ((3, 6), (3, 0), (0, 6), (0, 0))
PARAMS = pltpu.CompilerParams(vmem_limit_bytes=48 << 20)


def dot(a, b, ca=1, cb=0):
    return lax.dot_general(a, b, (((ca,), (cb,)), ((), ())), preferred_element_type=F32)


def selections():
    pack = np.zeros((320, 384), np.float32)
    gather = np.zeros((4, 288, 72), np.float32)
    leave = np.zeros((192, 144), np.float32)
    place = np.zeros((4, 192, 36), np.float32)
    for q, (a0, b0) in enumerate(QUADS):
        for p in range(2):
            for a in range(3):
                for b in range(6):
                    row = (p * 3 + a) * 6 + b
                    slab = (((p + 1) % 2) * 6 + a0 + a) * 16 + b0 + b
                    token = (p * 6 + (3 - a0) + a) * 12 + (6 - b0) + b
                    for arr in range(2):
                        pack[q * 80 + arr * 36 + row, arr * 192 + slab] = 1
                        gather[q, arr * 144 + token, arr * 36 + row] = 1
                    leave[q * 48 + row, token] = 1
                    place[q, slab, row] = 1
    return [jnp.asarray(m, BF16) for m in (pack, gather, leave, place)]


def pack_kernel(tok, cot, sel, own, lon, lat, diag, slabs):
    slabs[...] = jnp.zeros_like(slabs)
    for k in range(12):
        slabs[k, 0:12, :] = tok[k // 6, k % 6]
        slabs[12 + k, 0:12, :] = cot[k // 6, k % 6]
    out = dot(sel[...], slabs[...].reshape(384, C)).astype(BF16)
    own[...] = out[0:72]
    lon[...] = out[80:152]
    lat[...] = out[160:232]
    diag[...] = out[240:312]


def unpack_kernel(own, lon, lat, diag, sel, out):
    total = dot(sel[0], own[...])
    for q, ref in enumerate((lon, lat, diag)):
        total = total + dot(sel[q + 1], ref[...])
    slabs = total.astype(BF16).reshape(12, 16, C)
    for k in range(12):
        out[k // 6, k % 6] = slabs[k, 0:12]


def bias_kernel(idx, table, col, row, bias, packed, flat):
    packed[0:T, :] = idx[:, 0:128]
    lane = lax.broadcasted_iota(jnp.int32, (24, 128), 1)
    tail = jnp.zeros((24, 128), jnp.int32)
    for c in range(6):
        part = jnp.concatenate(
            (idx[24 * c : 24 * c + 24, 128:T], jnp.zeros((24, 112), jnp.int32)), axis=1
        )
        part = pltpu.roll(part, 16 * c, 1) if c else part
        tail = jnp.where((lane >= 16 * c) & (lane < 16 * c + 16), part, tail)
    packed[T:PACK, :] = tail

    def block(i, carry):
        at = pl.ds(pl.multiple_of(i * 8, 8), 8)
        position = packed[at, :]
        low = position & 127
        high = position >> 7
        for h in range(HEADS):
            total = jnp.zeros((8, 128), F32)
            for k in range(BLKS):
                r = h * BLKS + k
                values = jnp.broadcast_to(table[r : r + 1, :], (8, 128))
                found = jnp.take_along_axis(values, low, axis=1, mode="promise_in_bounds")
                total = jnp.where(high == k, found, total)
            flat[h, at, :] = total
        return carry

    lax.fori_loop(0, PACK // 8, block, 0)
    same = col[...] == row[...]
    for h in range(HEADS):
        bias[h, :, 0:128] = jnp.where(same[:, 0:128], flat[h, 0:T, :], -1e9)
        tail = flat[h, T:PACK, :]
        for c in range(6):
            part = pltpu.roll(tail, 128 - 16 * c, 1) if c else tail
            at = slice(24 * c, 24 * c + 24)
            bias[h, at, 128:T] = jnp.where(same[at, 128:T], part[:, 0:16], -1e9)


def main_kernel(own, lon, lat, diag, sel, bias, wqkv, wproj, leave,
                ret_own, ret_lon, ret_lat, ret_diag, grads, ds_out, ds_tail):
    scale = HD ** (-0.5)
    both = dot(sel[0], own[...])
    for q, ref in enumerate((lon, lat, diag)):
        both = both + dot(sel[q + 1], ref[...])
    values = both[0:T]
    cot32 = both[T:]
    cot = cot32.astype(BF16)
    center = values - jnp.mean(values, axis=-1, keepdims=True)
    inv_std = lax.rsqrt(jnp.mean(center * center, axis=-1, keepdims=True) + 1e-05)
    normed = center * inv_std
    hidden = normed.astype(BF16)
    proj = dot(hidden, wqkv[...])
    query = proj[:, 0:C]
    query_t = query.T.astype(BF16)
    query = query.astype(BF16)
    key = proj[:, C : 2 * C].astype(BF16)
    value = proj[:, 2 * C :].astype(BF16)
    att = dot(cot, wproj[...], 1, 1)
    att_t = att.T.astype(BF16)
    att = att.astype(BF16)
    head = lax.broadcasted_iota(jnp.int32, (T, C), 1) // HD
    zero = jnp.zeros((T, C), BF16)
    attended = jnp.zeros((T, C), F32)
    grad_query = jnp.zeros((T, C), F32)
    key_t = []
    value_t = []
    lane = lax.broadcasted_iota(jnp.int32, (24, 128), 1)
    for h in range(HEADS):
        mine = head == h
        scores = dot(jnp.where(mine, query, zero), key, 1, 1) * scale + bias[h]
        exponent = jnp.exp(scores - jnp.max(scores, axis=-1, keepdims=True))
        prob = exponent * (1.0 / jnp.sum(exponent, axis=-1, keepdims=True))
        prob_half = prob.astype(BF16)
        attended = attended + dot(prob_half, jnp.where(mine, value, zero))
        grad_prob = dot(jnp.where(mine, att, zero), value, 1, 1)
        value_t.append(dot(att_t[HD * h : HD * h + HD], prob_half))
        ds = prob * (grad_prob - jnp.sum(grad_prob * prob, axis=-1, keepdims=True))
        ds_half = ds.astype(BF16)
        grad_query = grad_query + dot(ds_half, jnp.where(mine, key, zero))
        key_t.append(dot(query_t[HD * h : HD * h + HD], ds_half))
        ds_out[h, 0:T, :] = ds[:, 0:128]
        ds_tail[:, 0:16] = ds[:, 128:T]
        packed = jnp.zeros((24, 128), F32)
        for c in range(6):
            part = ds_tail[24 * c : 24 * c + 24, :]
            part = pltpu.roll(part, 16 * c, 1) if c else part
            packed = jnp.where((lane >= 16 * c) & (lane < 16 * c + 16), part, packed)
        ds_out[h, T:PACK, :] = packed
    grad_key = jnp.concatenate(key_t, axis=0).T
    grad_value = jnp.concatenate(value_t, axis=0).T
    grad_in = jnp.concatenate((grad_query * scale, grad_key * scale, grad_value), axis=1)
    grad_in = grad_in.astype(BF16)
    grad_qkv = dot(hidden, grad_in, 0, 0)
    grad_proj = dot(attended.astype(BF16), cot, 0, 0)
    grads[...] = jnp.concatenate((grad_qkv, grad_proj), axis=1).astype(BF16)
    grad_hidden = dot(grad_in, wqkv[...], 1, 1)
    grad_norm = inv_std * (
        grad_hidden
        - jnp.mean(grad_hidden, axis=-1, keepdims=True)
        - normed * jnp.mean(grad_hidden * normed, axis=-1, keepdims=True)
    )
    returned = (cot32 + grad_norm).astype(BF16)
    parts = dot(leave[...], returned).astype(BF16)
    ret_own[...] = parts[0:36]
    ret_lon[...] = parts[48:84]
    ret_lat[...] = parts[96:132]
    ret_diag[...] = parts[144:180]


def scatter_kernel(idx, ds, out, packed, total):
    packed[0:T, :] = idx[:, 0:128]
    lane = lax.broadcasted_iota(jnp.int32, (24, 128), 1)
    tail = jnp.zeros((24, 128), jnp.int32)
    for c in range(6):
        part = jnp.concatenate(
            (idx[24 * c : 24 * c + 24, 128:T], jnp.zeros((24, 112), jnp.int32)), axis=1
        )
        part = pltpu.roll(part, 16 * c, 1) if c else part
        tail = jnp.where((lane >= 16 * c) & (lane < 16 * c + 16), part, tail)
    packed[T:PACK, :] = tail
    total[...] = jnp.zeros_like(total)
    blocks = lax.broadcasted_iota(jnp.int32, (32, 128), 0)
    lows = lax.broadcasted_iota(jnp.int32, (128, 128), 0)

    def block(i, carry):
        at = pl.ds(pl.multiple_of(i * 8, 8), 8)
        position = packed[at, :]
        low = position & 127
        high = position >> 7
        left = []
        right = []
        for r in range(8):
            right.append(jnp.where(lows == low[r : r + 1], 1.0, 0.0).astype(BF16))
            mine = blocks == high[r : r + 1]
            parts = []
            for h in range(HEADS):
                row = ds[h, at, :][r : r + 1]
                parts.append(jnp.where(mine, row, 0.0).astype(BF16))
            left.append(jnp.concatenate(parts, axis=0))
        total[...] += dot(jnp.concatenate(left, axis=1), jnp.concatenate(right, axis=1), 1, 1)
        return carry

    lax.fori_loop(0, PACK // 8, block, 0)
    out[...] = total[...].astype(BF16)


def call(kernel, shapes, scratch, cost, *args):
    return pl.pallas_call(
        kernel,
        out_shape=[jax.ShapeDtypeStruct(s, d) for s, d in shapes],
        scratch_shapes=[pltpu.VMEM(s, d) for s, d in scratch],
        compiler_params=PARAMS,
        cost_estimate=pl.CostEstimate(flops=cost, bytes_accessed=1 << 20, transcendentals=0),
    )(*args)


def exchange(block, axes, groups=None):
    return lax.all_to_all(block, axes, 0, 0, axis_index_groups=groups, tiled=False)


def summed(parts):
    return jnp.sum(parts.astype(F32), axis=0)


def local(sizes, tokens, cotangent, region, pos_index, w_qkv, w_proj, bias_table):
    n_lon, n_lat, n_y = sizes
    n_z = n_lon // n_y
    pack, gather, leave, place = selections()
    axes = ("lon", "lat", "rep")

    def moved(block, d_lon, d_lat):
        route = []
        for i in range(n_lon):
            for j in range(n_lat):
                source = ((i + d_lon) % n_lon) * n_lat + (j + d_lat) % n_lat
                route.append((source, i * n_lat + j))
        return lax.ppermute(block, axes, route)

    strip = ((72, C), BF16)
    own, lon, lat, diag = call(
        pack_kernel, [strip] * 4, [((24, 16, C), BF16)], 10**8, tokens, cotangent, pack
    )
    lon, lat, diag = moved(lon, 1, 0), moved(lat, 0, 1), moved(diag, 1, 1)

    table = jnp.pad(bias_table.reshape(ROWS, HEADS).T, ((0, 0), (0, BLKS * 128 - ROWS)))
    table = table.reshape(HEADS * BLKS, 128)
    (bias,) = call(
        bias_kernel,
        [((HEADS, T, T), F32)],
        [((PACK, 128), jnp.int32), ((HEADS, PACK, 128), F32)],
        5 * 10**9,
        pos_index,
        table,
        region.reshape(T, 1),
        region.reshape(1, T),
    )
    back = ((36, C), BF16)
    ret_own, ret_lon, ret_lat, ret_diag, grads, ds = call(
        main_kernel,
        [back] * 4 + [((C, 4 * C), BF16), ((HEADS, PACK, 128), F32)],
        [((T, 128), F32)],
        10**10,
        own, lon, lat, diag, gather, bias, w_qkv, w_proj, leave,
    )
    ret_lon, ret_lat, ret_diag = (
        moved(ret_lon, -1, 0), moved(ret_lat, 0, -1), moved(ret_diag, -1, -1),
    )
    across = ("lat", "rep")
    chunk = exchange(grads.reshape(n_lat, C // n_lat, 4 * C), across)
    (scattered,) = call(
        scatter_kernel,
        [((192, 128), BF16)],
        [((PACK, 128), jnp.int32), ((192, 128), F32)],
        5 * 10**9,
        pos_index,
        ds,
    )
    (grad_tokens,) = call(
        unpack_kernel, [((2, 6, 12, C), BF16)], [], 10**8,
        ret_own, ret_lon, ret_lat, ret_diag, place,
    )
    chunk = summed(chunk).astype(BF16)
    rows = chunk.size // 128
    mixed = jnp.concatenate(
        (chunk.reshape(n_y, rows // n_y, 128), scattered.reshape(n_y, 192 // n_y, 128)), axis=1
    )
    rows_y = [[z * n_y + y for y in range(n_y)] for z in range(n_z)]
    rows_z = [[z * n_y + y for z in range(n_z)] for y in range(n_y)]
    mixed = summed(exchange(mixed, "lon", rows_y)).astype(BF16)
    mixed = jnp.broadcast_to(mixed, (n_z,) + mixed.shape)
    mixed = summed(exchange(mixed, "lon", rows_z)).astype(BF16)
    mixed = jnp.broadcast_to(mixed, (n_y,) + mixed.shape)
    mixed = exchange(mixed, "lon", rows_y)
    chunk = mixed[:, : rows // n_y].reshape(C // n_lat, 4 * C)
    scattered = mixed[:, rows // n_y :].reshape(HEADS, 32 * 128)
    grad_bias = scattered[:, :ROWS].astype(F32).T.reshape(ROWS, 1, HEADS)
    grads = exchange(jnp.broadcast_to(chunk, (n_lat,) + chunk.shape), across)
    grads = grads.reshape(C, 4 * C).astype(F32)
    return (grad_tokens, grads[:, : 3 * C], grads[:, 3 * C :], grad_bias)


def solution(mesh):
    n_lon = mesh.shape["lon"]
    n_lat = mesh.shape["lat"] * mesh.shape["rep"]
    n_y = 8 if n_lon % 8 == 0 else 2
    placed = (
        P(None, ("lat", "rep"), "lon", None),
        P(None, ("lat", "rep"), "lon", None),
        P(None, ("lat", "rep"), "lon"),
        P(),
        P(),
        P(),
        P(None, ("lat", "rep"), None),
    )
    return jax.shard_map(
        functools.partial(local, (n_lon, n_lat, n_y)),
        mesh=mesh,
        in_specs=placed,
        out_specs=(P(None, ("lat", "rep"), "lon", None), P(), P(), P(None, ("lat", "rep"), None)),
        check_vma=False,
    )
```

```python
import functools

import jax
import jax.numpy as jnp
import numpy as np
from jax import lax
from jax.experimental import pallas as pl
from jax.experimental.pallas import tpu as pltpu
from jax.sharding import PartitionSpec as P

F32 = jnp.float32
BF16 = jnp.bfloat16
T = 144
C = 192
HEADS = 6
HD = 32
ROWS = 3312
BLKS = 26
PACK = 168
HALF = HEADS // 2
PARAMS = pltpu.CompilerParams(vmem_limit_bytes=48 << 20)


def dot(a, b, ca=1, cb=0):
    return lax.dot_general(a, b, (((ca,), (cb,)), ((), ())), preferred_element_type=F32)


def selections():
    first = np.zeros((288, 384), np.float32)
    second = np.zeros((2, 144, 144), np.float32)
    gather = np.zeros((3, 288, 144), np.float32)
    leave = np.zeros((160, 144), np.float32)
    place = np.zeros((4, 192, 40), np.float32)
    for p in range(2):
        for a in range(6):
            for b in range(12):
                slab = (((p + 1) % 2) * 6 + a) * 16 + b
                half = (p * 6 + a) * 6 + b % 6
                wide = (p * 3 + a % 3) * 12 + (b + 6) % 12
                for arr in range(2):
                    first[(0 if b < 6 else 144) + arr * 72 + half, arr * 192 + slab] = 1
                    source = 1 if b < 6 else 0
                    if a < 3:
                        second[source, arr * 72 + wide, arr * 72 + half] = 1
                    else:
                        token = (p * 6 + a - 3) * 12 + (b + 6) % 12
                        gather[source, arr * 144 + token, arr * 72 + half] = 1
                token = (p * 6 + a) * 12 + b
                if a >= 3:
                    for arr in range(2):
                        row = (p * 3 + a - 3) * 12 + b
                        gather[2, arr * 144 + token, arr * 72 + row] = 1
                row = (p * 3 + a % 3) * 6 + b % 6
                leave[(80 if a >= 3 else 0) + (40 if b >= 6 else 0) + row, token] = 1
                home = (((p + 1) % 2) * 6 + (a + 3) % 6) * 16 + (b + 6) % 12
                place[(2 if b >= 6 else 0) + (1 if a >= 3 else 0), home, row] = 1
    return [jnp.asarray(m, BF16) for m in (first, second, gather, leave, place)]


def pack_kernel(tok, cot, sel, strip, kept, slabs):
    slabs[...] = jnp.zeros_like(slabs)
    for k in range(12):
        slabs[k, 0:12, :] = tok[k // 6, k % 6]
        slabs[12 + k, 0:12, :] = cot[k // 6, k % 6]
    out = dot(sel[...], slabs[...].reshape(384, C)).astype(BF16)
    strip[...] = out[0:T]
    kept[...] = out[T:]


def repack_kernel(kept, arrived, sel, strip):
    strip[...] = (dot(sel[0], kept[...]) + dot(sel[1], arrived[...])).astype(BF16)


def unpack_kernel(kept, first, second, sel, out):
    total = dot(sel[0], kept[0]) + dot(sel[1], first[0])
    total = total + dot(sel[2], second[0]) + dot(sel[3], second[1])
    slabs = total.astype(BF16).reshape(12, 16, C)
    for k in range(12):
        out[k // 6, k % 6] = slabs[k, 0:12]


def finish_kernel(parts, qkv, proj):
    n, rows, _ = parts.shape
    for k in range(n):
        part = parts[k].astype(F32)
        qkv[rows * k : rows * k + rows, :] = part[:, : 3 * C]
        proj[rows * k : rows * k + rows, :] = part[:, 3 * C :]


def bias_kernel(first, idx, table, col, row, bias, packed, flat):
    packed[0:T, :] = idx[:, 0:128]
    lane = lax.broadcasted_iota(jnp.int32, (24, 128), 1)
    tail = jnp.zeros((24, 128), jnp.int32)
    for c in range(6):
        part = jnp.concatenate(
            (idx[24 * c : 24 * c + 24, 128:T], jnp.zeros((24, 112), jnp.int32)), axis=1
        )
        part = pltpu.roll(part, 16 * c, 1) if c else part
        tail = jnp.where((lane >= 16 * c) & (lane < 16 * c + 16), part, tail)
    packed[T:PACK, :] = tail

    def block(i, carry):
        at = pl.ds(pl.multiple_of(i * 8, 8), 8)
        position = packed[at, :]
        low = position & 127
        high = position >> 7
        for h in range(HALF):
            total = jnp.zeros((8, 128), F32)
            for k in range(BLKS):
                r = (first + h) * BLKS + k
                values = jnp.broadcast_to(table[r : r + 1, :], (8, 128))
                found = jnp.take_along_axis(values, low, axis=1, mode="promise_in_bounds")
                total = jnp.where(high == k, found, total)
            flat[h, at, :] = total
        return carry

    lax.fori_loop(0, PACK // 8, block, 0)
    same = col[...] == row[...]
    for h in range(HALF):
        bias[h, :, 0:128] = jnp.where(same[:, 0:128], flat[h, 0:T, :], -1e9)
        tail = flat[h, T:PACK, :]
        for c in range(6):
            part = pltpu.roll(tail, 128 - 16 * c, 1) if c else tail
            at = slice(24 * c, 24 * c + 24)
            bias[h, at, 128:T] = jnp.where(same[at, 128:T], part[:, 0:16], -1e9)


def main_kernel(kept, lon, lat, sel, bias_a, bias_b, wqkv, wproj, leave,
                ret_kept, ret_strip, grads, ds_out, ds_tail):
    scale = HD ** (-0.5)
    both = dot(sel[0], kept[...]) + dot(sel[1], lon[...]) + dot(sel[2], lat[...])
    values = both[0:T]
    cot32 = both[T:]
    cot = cot32.astype(BF16)
    center = values - jnp.mean(values, axis=-1, keepdims=True)
    inv_std = lax.rsqrt(jnp.mean(center * center, axis=-1, keepdims=True) + 1e-05)
    normed = center * inv_std
    hidden = normed.astype(BF16)
    proj = dot(hidden, wqkv[...])
    query = proj[:, 0:C]
    query_t = query.T.astype(BF16)
    query = query.astype(BF16)
    key = proj[:, C : 2 * C].astype(BF16)
    value = proj[:, 2 * C :].astype(BF16)
    att = dot(cot, wproj[...], 1, 1)
    att_t = att.T.astype(BF16)
    att = att.astype(BF16)
    head = lax.broadcasted_iota(jnp.int32, (T, C), 1) // HD
    zero = jnp.zeros((T, C), BF16)
    attended = jnp.zeros((T, C), F32)
    grad_query = jnp.zeros((T, C), F32)
    key_t = []
    value_t = []
    lane = lax.broadcasted_iota(jnp.int32, (24, 128), 1)
    for h in range(HEADS):
        mine = head == h
        scores = dot(jnp.where(mine, query, zero), key, 1, 1) * scale
        scores = scores + (bias_a[h] if h < HALF else bias_b[h - HALF])
        exponent = jnp.exp(scores - jnp.max(scores, axis=-1, keepdims=True))
        prob = exponent * (1.0 / jnp.sum(exponent, axis=-1, keepdims=True))
        prob_half = prob.astype(BF16)
        attended = attended + dot(prob_half, jnp.where(mine, value, zero))
        grad_prob = dot(jnp.where(mine, att, zero), value, 1, 1)
        value_t.append(dot(att_t[HD * h : HD * h + HD], prob_half))
        ds = prob * (grad_prob - jnp.sum(grad_prob * prob, axis=-1, keepdims=True))
        ds_half = ds.astype(BF16)
        grad_query = grad_query + dot(ds_half, jnp.where(mine, key, zero))
        key_t.append(dot(query_t[HD * h : HD * h + HD], ds_half))
        ds_out[h, 0:T, :] = ds[:, 0:128]
        ds_tail[:, 0:16] = ds[:, 128:T]
        packed = jnp.zeros((24, 128), F32)
        for c in range(6):
            part = ds_tail[24 * c : 24 * c + 24, :]
            part = pltpu.roll(part, 16 * c, 1) if c else part
            packed = jnp.where((lane >= 16 * c) & (lane < 16 * c + 16), part, packed)
        ds_out[h, T:PACK, :] = packed
    grad_key = jnp.concatenate(key_t, axis=0).T
    grad_value = jnp.concatenate(value_t, axis=0).T
    grad_in = jnp.concatenate((grad_query * scale, grad_key * scale, grad_value), axis=1)
    grad_in = grad_in.astype(BF16)
    grad_qkv = dot(hidden, grad_in, 0, 0)
    grad_proj = dot(attended.astype(BF16), cot, 0, 0)
    grads[...] = jnp.concatenate((grad_qkv, grad_proj), axis=1).astype(BF16)
    grad_hidden = dot(grad_in, wqkv[...], 1, 1)
    grad_norm = inv_std * (
        grad_hidden
        - jnp.mean(grad_hidden, axis=-1, keepdims=True)
        - normed * jnp.mean(grad_hidden * normed, axis=-1, keepdims=True)
    )
    returned = (cot32 + grad_norm).astype(BF16)
    parts = dot(leave[...], returned).astype(BF16)
    for k in range(2):
        ret_kept[k] = parts[40 * k : 40 * k + 40]
        ret_strip[k] = parts[80 + 40 * k : 120 + 40 * k]


def scatter_kernel(idx, ds, out, packed, total):
    packed[0:T, :] = idx[:, 0:128]
    lane = lax.broadcasted_iota(jnp.int32, (24, 128), 1)
    tail = jnp.zeros((24, 128), jnp.int32)
    for c in range(6):
        part = jnp.concatenate(
            (idx[24 * c : 24 * c + 24, 128:T], jnp.zeros((24, 112), jnp.int32)), axis=1
        )
        part = pltpu.roll(part, 16 * c, 1) if c else part
        tail = jnp.where((lane >= 16 * c) & (lane < 16 * c + 16), part, tail)
    packed[T:PACK, :] = tail
    total[...] = jnp.zeros_like(total)
    blocks = lax.broadcasted_iota(jnp.int32, (32, 128), 0)
    lows = lax.broadcasted_iota(jnp.int32, (128, 128), 0)

    def block(i, carry):
        at = pl.ds(pl.multiple_of(i * 8, 8), 8)
        position = packed[at, :]
        low = position & 127
        high = position >> 7
        left = []
        right = []
        for r in range(8):
            right.append(jnp.where(lows == low[r : r + 1], 1.0, 0.0).astype(BF16))
            mine = blocks == high[r : r + 1]
            parts = []
            for h in range(HEADS):
                row = ds[h, at, :][r : r + 1]
                parts.append(jnp.where(mine, row, 0.0).astype(BF16))
            left.append(jnp.concatenate(parts, axis=0))
        total[...] += dot(jnp.concatenate(left, axis=1), jnp.concatenate(right, axis=1), 1, 1)
        return carry

    lax.fori_loop(0, PACK // 8, block, 0)
    out[...] = total[...].astype(BF16)


def call(kernel, shapes, scratch, cost, *args):
    return pl.pallas_call(
        kernel,
        out_shape=[jax.ShapeDtypeStruct(s, d) for s, d in shapes],
        scratch_shapes=[pltpu.VMEM(s, d) for s, d in scratch],
        compiler_params=PARAMS,
        cost_estimate=pl.CostEstimate(flops=cost, bytes_accessed=1 << 20, transcendentals=0),
    )(*args)


def exchange(block, axes, groups=None):
    return lax.all_to_all(block, axes, 0, 0, axis_index_groups=groups, tiled=False)


def summed(parts):
    return jnp.sum(parts.astype(F32), axis=0)


def local(sizes, tokens, cotangent, region, pos_index, w_qkv, w_proj, bias_table):
    n_lon, n_lat, n_y = sizes
    n_z = n_lon // n_y
    first, second, gather, leave, place = selections()
    across = ("lat", "rep")

    def moved(block, axes, n, distance):
        return lax.ppermute(block, axes, [((i + distance) % n, i) for i in range(n)])

    table = jnp.pad(bias_table.reshape(ROWS, HEADS).T, ((0, 0), (0, BLKS * 128 - ROWS)))
    table = table.reshape(HEADS * BLKS, 128)

    def bias_of(head, index):
        (bias,) = call(
            functools.partial(bias_kernel, head),
            [((HALF, T, T), F32)],
            [((PACK, 128), jnp.int32), ((HALF, PACK, 128), F32)],
            3 * 10**9,
            index,
            table,
            region.reshape(T, 1),
            region.reshape(1, T),
        )
        return bias

    block = ((T, C), BF16)
    strip, kept = call(
        pack_kernel, [block] * 2, [((24, 16, C), BF16)], 10**8, tokens, cotangent, first
    )
    lon = moved(strip, "lon", n_lon, 1)
    bias_a = bias_of(0, pos_index)
    (strip,) = call(repack_kernel, [block], [], 10**8, kept, lon, second)
    strip, late_index = lax.optimization_barrier((strip, pos_index))
    lat = moved(strip, across, n_lat, 1)
    bias_b = bias_of(HALF, late_index)
    quarter = ((2, 40, C), BF16)
    ret_kept, ret_strip, grads, ds = call(
        main_kernel,
        [quarter] * 2 + [((C, 4 * C), BF16), ((HEADS, PACK, 128), F32)],
        [((T, 128), F32)],
        10**10,
        kept, lon, lat, gather, bias_a, bias_b, w_qkv, w_proj, leave,
    )
    chunk = exchange(grads.reshape(n_lat, C // n_lat, 4 * C), across)
    (scattered,) = call(
        scatter_kernel,
        [((192, 128), BF16)],
        [((PACK, 128), jnp.int32), ((192, 128), F32)],
        5 * 10**9,
        pos_index,
        ds,
    )
    chunk = summed(chunk).astype(BF16)
    rows = chunk.size // 128
    mixed = jnp.concatenate(
        (chunk.reshape(n_y, rows // n_y, 128), scattered.reshape(n_y, 192 // n_y, 128)), axis=1
    )
    rows_y = [[z * n_y + y for y in range(n_y)] for z in range(n_z)]
    rows_z = [[z * n_y + y for z in range(n_z)] for y in range(n_y)]
    mixed, ret_strip = lax.optimization_barrier((mixed, ret_strip))
    ret_first = moved(ret_strip, across, n_lat, -1)
    mixed = summed(exchange(mixed, "lon", rows_y)).astype(BF16)
    mixed = jnp.broadcast_to(mixed, (n_z,) + mixed.shape)
    mixed, ret_first = lax.optimization_barrier((mixed, ret_first))
    ret_second = moved(jnp.stack((ret_kept[1], ret_first[1])), "lon", n_lon, -1)
    mixed = summed(exchange(mixed, "lon", rows_z)).astype(BF16)
    mixed = jnp.broadcast_to(mixed, (n_y,) + mixed.shape)
    mixed, ret_second = lax.optimization_barrier((mixed, ret_second))
    (grad_tokens,) = call(
        unpack_kernel, [((2, 6, 12, C), BF16)], [], 10**8, ret_kept, ret_first, ret_second, place,
    )
    mixed = exchange(mixed, "lon", rows_y)
    chunk = mixed[:, : rows // n_y].reshape(C // n_lat, 4 * C)
    scattered = mixed[:, rows // n_y :].reshape(HEADS, 32 * 128)
    grads = exchange(jnp.broadcast_to(chunk, (n_lat,) + chunk.shape), across)
    grad_qkv, grad_proj = call(
        finish_kernel, [((C, 3 * C), F32), ((C, C), F32)], [], 10**7, grads
    )
    grad_bias = scattered[:, :ROWS].astype(F32).T.reshape(ROWS, 1, HEADS)
    return (grad_tokens, grad_qkv, grad_proj, grad_bias)


def solution(mesh):
    n_lon = mesh.shape["lon"]
    n_lat = mesh.shape["lat"] * mesh.shape["rep"]
    n_y = 8 if n_lon % 8 == 0 else 2
    placed = (
        P(None, ("lat", "rep"), "lon", None),
        P(None, ("lat", "rep"), "lon", None),
        P(None, ("lat", "rep"), "lon"),
        P(),
        P(),
        P(),
        P(None, ("lat", "rep"), None),
    )
    return jax.shard_map(
        functools.partial(local, (n_lon, n_lat, n_y)),
        mesh=mesh,
        in_specs=placed,
        out_specs=(P(None, ("lat", "rep"), "lon", None), P(), P(), P(None, ("lat", "rep"), None)),
        check_vma=False,
    )
```

```python
import functools

import jax
import jax.numpy as jnp
import numpy as np
from jax import lax
from jax.experimental import pallas as pl
from jax.experimental.pallas import tpu as pltpu
from jax.sharding import PartitionSpec as P

F32 = jnp.float32
BF16 = jnp.bfloat16
T = 144
C = 192
HEADS = 6
HD = 32
ROWS = 3312
BLKS = 26
PACK = 168
HALF = HEADS // 2
PARAMS = pltpu.CompilerParams(vmem_limit_bytes=48 << 20)


def dot(a, b, ca=1, cb=0):
    return lax.dot_general(a, b, (((ca,), (cb,)), ((), ())), preferred_element_type=F32)


def selections():
    first = np.zeros((288, 288), np.float32)
    second = np.zeros((2, 144, 144), np.float32)
    gather = np.zeros((3, 288, 144), np.float32)
    leave = np.zeros((160, 144), np.float32)
    place = np.zeros((4, T, 40), np.float32)
    for p in range(2):
        for a in range(6):
            for b in range(12):
                slab = (a * 12 + b) * 2 + (p + 1) % 2
                half = (p * 6 + a) * 6 + b % 6
                wide = (p * 3 + a % 3) * 12 + (b + 6) % 12
                for arr in range(2):
                    first[(0 if b < 6 else 144) + arr * 72 + half, arr * T + slab] = 1
                    source = 1 if b < 6 else 0
                    if a < 3:
                        second[source, arr * 72 + wide, arr * 72 + half] = 1
                    else:
                        token = (p * 6 + a - 3) * 12 + (b + 6) % 12
                        gather[source, arr * 144 + token, arr * 72 + half] = 1
                token = (p * 6 + a) * 12 + b
                if a >= 3:
                    for arr in range(2):
                        row = (p * 3 + a - 3) * 12 + b
                        gather[2, arr * 144 + token, arr * 72 + row] = 1
                row = (p * 3 + a % 3) * 6 + b % 6
                leave[(80 if a >= 3 else 0) + (40 if b >= 6 else 0) + row, token] = 1
                home = (((a + 3) % 6) * 12 + (b + 6) % 12) * 2 + (p + 1) % 2
                place[(2 if b >= 6 else 0) + (1 if a >= 3 else 0), home, row] = 1
    return [jnp.asarray(m, BF16) for m in (first, second, gather, leave, place)]


def pack_kernel(tok, cot, sel, strip, kept, rows):
    for arr, ref in enumerate((tok, cot)):
        for k in range(72):
            at = arr * T + 2 * k
            rows[at : at + 2, :] = ref[k // 12, k % 12].astype(F32)
    out = dot(sel[...], rows[...].astype(BF16)).astype(BF16)
    strip[...] = out[0:T]
    kept[...] = out[T:]


def repack_kernel(kept, arrived, sel, strip):
    strip[...] = (dot(sel[0], kept[...]) + dot(sel[1], arrived[...])).astype(BF16)


def unpack_kernel(kept, first, second, sel, out, rows):
    total = dot(sel[0], kept[0]) + dot(sel[1], first[0])
    rows[...] = total + dot(sel[2], second[0]) + dot(sel[3], second[1])
    for k in range(72):
        out[k // 12, k % 12] = rows[2 * k : 2 * k + 2, :].astype(BF16)


def mix_kernel(parts, scattered, out, wide):
    n, rows, _ = out.shape
    bias_rows = scattered.shape[0] // n
    rows = rows - bias_rows
    wide[...] = jnp.sum(parts[...].astype(F32), axis=0)
    for k in range(n):
        mine = wide[rows * k : rows * k + rows, :]
        theirs = scattered[bias_rows * k : bias_rows * k + bias_rows, :]
        out[k] = jnp.concatenate((mine, theirs), axis=0).astype(BF16)


def sum_kernel(parts, out):
    total = jnp.sum(parts[...].astype(F32), axis=0).astype(BF16)
    for k in range(out.shape[0]):
        out[k] = total


def split_kernel(parts, out, scattered, wide):
    n = parts.shape[0]
    bias_rows = scattered.shape[0] // n
    rows = parts.shape[1] - bias_rows
    for k in range(n):
        part = parts[k].astype(F32)
        wide[rows * k : rows * k + rows, :] = part[0:rows]
        scattered[bias_rows * k : bias_rows * k + bias_rows, :] = part[rows:]
    total = wide[...].astype(BF16)
    for k in range(out.shape[0]):
        out[k] = total


def finish_kernel(parts, qkv, proj):
    wide = parts[...].reshape(6 * C, 128).astype(F32)
    for k in range(4):
        qkv[:, 128 * k : 128 * k + 128] = wide[C * k : C * k + C]
    qkv[:, 512:576] = wide[4 * C : 5 * C, 0:64]
    proj[:, 0:64] = wide[4 * C : 5 * C, 64:128]
    proj[:, 64:C] = wide[5 * C : 6 * C]


def packed_rows(idx):
    lane = lax.broadcasted_iota(jnp.int32, (24, 128), 1)
    tail = jnp.zeros((24, 128), jnp.int32)
    for c in range(6):
        part = jnp.concatenate(
            (idx[24 * c : 24 * c + 24, 128:T], jnp.zeros((24, 112), jnp.int32)), axis=1
        )
        part = pltpu.roll(part, 16 * c, 1) if c else part
        tail = jnp.where((lane >= 16 * c) & (lane < 16 * c + 16), part, tail)
    return tail


def bias_body(first, table, col, row, packed, bias, flat):
    def block(i, carry):
        at = pl.ds(pl.multiple_of(i * 8, 8), 8)
        position = packed[at, :]
        low = position & 127
        high = position >> 7
        totals = [jnp.zeros((8, 128), F32)] * HALF
        for k in range(BLKS):
            here = high == k
            for h in range(HALF):
                r = (first + h) * BLKS + k
                values = jnp.broadcast_to(table[r : r + 1, :], (8, 128))
                found = jnp.take_along_axis(values, low, axis=1, mode="promise_in_bounds")
                totals[h] = jnp.where(here, found, totals[h])
        for h in range(HALF):
            flat[h, at, :] = totals[h]
        return carry

    lax.fori_loop(0, PACK // 8, block, 0)
    same = col[...] == row[...]
    for h in range(HALF):
        bias[h, :, 0:128] = jnp.where(same[:, 0:128], flat[h, 0:T, :], -1e9)
        tail = flat[h, T:PACK, :]
        for c in range(6):
            part = pltpu.roll(tail, 128 - 16 * c, 1) if c else tail
            at = slice(24 * c, 24 * c + 24)
            bias[h, at, 128:T] = jnp.where(same[at, 128:T], part[:, 0:16], -1e9)


def bias_first_kernel(idx, table, col, row, bias, packed, flat):
    packed[0:T, :] = idx[:, 0:128]
    packed[T:PACK, :] = packed_rows(idx)
    bias_body(0, table, col, row, packed, bias, flat)


def bias_second_kernel(packed, table, col, row, bias, flat):
    bias_body(HALF, table, col, row, packed, bias, flat)


def main_kernel(kept, lon, lat, sel, bias_a, bias_b, wqkv, wproj,
                grads, ds_out, grad_in_out, normed_out, inv_std_out, cot_out, ds_tail):
    scale = HD ** (-0.5)
    both = dot(sel[0], kept[...]) + dot(sel[1], lon[...]) + dot(sel[2], lat[...])
    values = both[0:T]
    cot = both[T:].astype(BF16)
    center = values - jnp.mean(values, axis=-1, keepdims=True)
    inv_std = lax.rsqrt(jnp.mean(center * center, axis=-1, keepdims=True) + 1e-05)
    normed = center * inv_std
    hidden = normed.astype(BF16)
    proj = dot(hidden, wqkv[...])
    query = proj[:, 0:C]
    query_t = query.T.astype(BF16)
    query = query.astype(BF16)
    key = proj[:, C : 2 * C].astype(BF16)
    value = proj[:, 2 * C :].astype(BF16)
    att = dot(cot, wproj[...], 1, 1)
    att_t = att.T.astype(BF16)
    att = att.astype(BF16)
    head = lax.broadcasted_iota(jnp.int32, (T, C), 1) // HD
    zero = jnp.zeros((T, C), BF16)
    attended = jnp.zeros((T, C), F32)
    grad_query = jnp.zeros((T, C), F32)
    key_t = []
    value_t = []
    lane = lax.broadcasted_iota(jnp.int32, (24, 128), 1)
    for h in range(HEADS):
        mine = head == h
        scores = dot(jnp.where(mine, query, zero), key, 1, 1) * scale
        scores = scores + (bias_a[h] if h < HALF else bias_b[h - HALF])
        exponent = jnp.exp(scores - jnp.max(scores, axis=-1, keepdims=True))
        prob = exponent * (1.0 / jnp.sum(exponent, axis=-1, keepdims=True))
        prob_half = prob.astype(BF16)
        attended = attended + dot(prob_half, jnp.where(mine, value, zero))
        grad_prob = dot(jnp.where(mine, att, zero), value, 1, 1)
        value_t.append(dot(att_t[HD * h : HD * h + HD], prob_half))
        ds = prob * (grad_prob - jnp.sum(grad_prob * prob, axis=-1, keepdims=True))
        ds_half = ds.astype(BF16)
        grad_query = grad_query + dot(ds_half, jnp.where(mine, key, zero))
        key_t.append(dot(query_t[HD * h : HD * h + HD], ds_half))
        ds_out[h, 0:T, :] = ds[:, 0:128]
        ds_tail[:, 0:16] = ds[:, 128:T]
        packed = jnp.zeros((24, 128), F32)
        for c in range(6):
            part = ds_tail[24 * c : 24 * c + 24, :]
            part = pltpu.roll(part, 16 * c, 1) if c else part
            packed = jnp.where((lane >= 16 * c) & (lane < 16 * c + 16), part, packed)
        ds_out[h, T:PACK, :] = packed
    grad_key = jnp.concatenate(key_t, axis=0).T
    grad_value = jnp.concatenate(value_t, axis=0).T
    grad_in = jnp.concatenate((grad_query * scale, grad_key * scale, grad_value), axis=1)
    grad_in = grad_in.astype(BF16)
    grad_qkv = dot(hidden, grad_in, 0, 0)
    grad_proj = dot(attended.astype(BF16), cot, 0, 0)
    both = jnp.concatenate((grad_qkv, grad_proj), axis=1).astype(BF16)
    for k in range(6):
        grads[C * k : C * k + C, :] = both[:, 128 * k : 128 * k + 128]
    grad_in_out[...] = grad_in
    normed_out[...] = normed
    inv_std_out[...] = inv_std
    cot_out[...] = cot


def norm_kernel(grad_in, normed_ref, inv_std, cot, wqkv, leave, ret_kept, ret_strip):
    normed = normed_ref[...]
    grad_hidden = dot(grad_in[...], wqkv[...], 1, 1)
    grad_norm = inv_std[...] * (
        grad_hidden
        - jnp.mean(grad_hidden, axis=-1, keepdims=True)
        - normed * jnp.mean(grad_hidden * normed, axis=-1, keepdims=True)
    )
    returned = (cot[...].astype(F32) + grad_norm).astype(BF16)
    parts = dot(leave[...], returned).astype(BF16)
    for k in range(2):
        ret_kept[k] = parts[40 * k : 40 * k + 40]
        ret_strip[k] = parts[80 + 40 * k : 120 + 40 * k]


def scatter_kernel(packed, ds, out, total):
    total[...] = jnp.zeros_like(total)
    blocks = lax.broadcasted_iota(jnp.int32, (32, 128), 0)
    lows = lax.broadcasted_iota(jnp.int32, (128, 128), 0)

    def block(i, carry):
        at = pl.ds(pl.multiple_of(i * 8, 8), 8)
        position = packed[at, :]
        low = position & 127
        high = position >> 7
        left = []
        right = []
        for r in range(8):
            right.append(jnp.where(lows == low[r : r + 1], 1.0, 0.0).astype(BF16))
            mine = blocks == high[r : r + 1]
            parts = []
            for h in range(HEADS):
                row = ds[h, at, :][r : r + 1]
                parts.append(jnp.where(mine, row, 0.0).astype(BF16))
            left.append(jnp.concatenate(parts, axis=0))
        total[...] += dot(jnp.concatenate(left, axis=1), jnp.concatenate(right, axis=1), 1, 1)
        return carry

    lax.fori_loop(0, PACK // 8, block, 0)
    out[...] = total[...]


def call(kernel, shapes, scratch, cost, *args):
    return pl.pallas_call(
        kernel,
        out_shape=[jax.ShapeDtypeStruct(s, d) for s, d in shapes],
        scratch_shapes=[pltpu.VMEM(s, d) for s, d in scratch],
        compiler_params=PARAMS,
        cost_estimate=pl.CostEstimate(flops=cost, bytes_accessed=1 << 20, transcendentals=0),
    )(*args)


def exchange(block, axes, groups=None):
    return lax.all_to_all(block, axes, 0, 0, axis_index_groups=groups, tiled=False)


def local(sizes, tokens, cotangent, region, pos_index, w_qkv, w_proj, bias_table):
    n_lon, n_lat, n_y = sizes
    n_z = n_lon // n_y
    first, second, gather, leave, place = selections()
    across = ("lat", "rep")

    def moved(block, axes, n, distance):
        return lax.ppermute(block, axes, [((i + distance) % n, i) for i in range(n)])

    table = jnp.pad(bias_table.reshape(ROWS, HEADS).T, ((0, 0), (0, BLKS * 128 - ROWS)))
    table = table.reshape(HEADS * BLKS, 128)

    col, row = region.reshape(T, 1), region.reshape(1, T)
    bias_shape = ((HALF, T, T), F32)
    bias_scratch = [((HALF, PACK, 128), F32)]
    block = ((T, C), BF16)
    order = (1, 2, 0, 3)
    strip, kept = call(
        pack_kernel, [block] * 2, [((2 * T, C), F32)], 10**8,
        tokens.transpose(order), cotangent.transpose(order), first,
    )
    lon = moved(strip, "lon", n_lon, 1)
    bias_a, packed = call(
        bias_first_kernel, [bias_shape, ((PACK, 128), jnp.int32)], bias_scratch, 3 * 10**9,
        pos_index, table, col, row,
    )
    (strip,) = call(repack_kernel, [block], [], 10**8, kept, lon, second)
    strip, late_packed = lax.optimization_barrier((strip, packed))
    lat = moved(strip, across, n_lat, 1)
    (bias_b,) = call(
        bias_second_kernel, [bias_shape], bias_scratch, 3 * 10**9, late_packed, table, col, row
    )
    grads, ds, grad_in, normed, inv_std, cot = call(
        main_kernel,
        [
            ((6 * C, 128), BF16),
            ((HEADS, PACK, 128), F32),
            ((T, 3 * C), BF16),
            ((T, C), F32),
            ((T, 1), F32),
            block,
        ],
        [((T, 128), F32)],
        10**10,
        kept, lon, lat, gather, bias_a, bias_b, w_qkv, w_proj,
    )
    rows_y = [[z * n_y + y for y in range(n_y)] for z in range(n_z)]
    rows_z = [[z * n_y + y for z in range(n_z)] for y in range(n_y)]
    rows = 6 * C // n_lat
    grads = exchange(grads.reshape(n_lat, rows, 128), across)
    (scattered,) = call(
        scatter_kernel, [((192, 128), F32)], [((192, 128), F32)], 5 * 10**9, packed, ds
    )
    mixed_rows = (rows + 192) // n_y
    wide = [((rows, 128), F32)]
    (mixed,) = call(
        mix_kernel, [((n_y, mixed_rows, 128), BF16)], wide, 10**7, grads, scattered
    )
    mixed, grad_in = lax.optimization_barrier((mixed, grad_in))
    quarter = ((2, 40, C), BF16)
    ret_kept, ret_strip = call(
        norm_kernel, [quarter] * 2, [], 10**8, grad_in, normed, inv_std, cot, w_qkv, leave
    )
    ret_first = moved(ret_strip, across, n_lat, -1)
    mixed = exchange(mixed, "lon", rows_y)
    (mixed,) = call(sum_kernel, [((n_z, mixed_rows, 128), BF16)], [], 10**7, mixed)
    mixed = exchange(mixed, "lon", rows_z)
    (mixed,) = call(sum_kernel, [((n_y, mixed_rows, 128), BF16)], [], 10**7, mixed)
    mixed, ret_first = lax.optimization_barrier((mixed, ret_first))
    ret_second = moved(jnp.stack((ret_kept[1], ret_first[1])), "lon", n_lon, -1)
    mixed = exchange(mixed, "lon", rows_y)
    grads, scattered = call(
        split_kernel, [((n_lat, rows, 128), BF16), ((192, 128), F32)], wide, 10**7, mixed
    )
    grads, ret_second = lax.optimization_barrier((grads, ret_second))
    grads = exchange(grads, across)
    (grad_tokens,) = call(
        unpack_kernel, [((6, 12, 2, C), BF16)], [((T, C), F32)], 10**8,
        ret_kept, ret_first, ret_second, place,
    )
    scattered = scattered.reshape(HEADS, 32 * 128)
    grad_bias = scattered[:, :ROWS].T.reshape(ROWS, 1, HEADS)
    grad_qkv, grad_proj = call(
        finish_kernel, [((C, 3 * C), F32), ((C, C), F32)], [], 10**7, grads
    )
    return (grad_tokens.transpose(2, 0, 1, 3), grad_qkv, grad_proj, grad_bias)


def solution(mesh):
    n_lon = mesh.shape["lon"]
    n_lat = mesh.shape["lat"] * mesh.shape["rep"]
    n_y = 8 if n_lon % 8 == 0 else 2
    placed = (
        P(None, ("lat", "rep"), "lon", None),
        P(None, ("lat", "rep"), "lon", None),
        P(None, ("lat", "rep"), "lon"),
        P(),
        P(),
        P(),
        P(None, ("lat", "rep"), None),
    )
    return jax.shard_map(
        functools.partial(local, (n_lon, n_lat, n_y)),
        mesh=mesh,
        in_specs=placed,
        out_specs=(P(None, ("lat", "rep"), "lon", None), P(), P(), P(None, ("lat", "rep"), None)),
        check_vma=False,
    )
```

```python
import functools

import jax
import jax.numpy as jnp
import numpy as np
from jax import lax
from jax.experimental import pallas as pl
from jax.experimental.pallas import tpu as pltpu
from jax.sharding import PartitionSpec as P

F32 = jnp.float32
BF16 = jnp.bfloat16
T = 144
C = 192
HEADS = 6
HD = 32
ROWS = 3312
BLKS = 26
PACK = 168
HALF = HEADS // 2


def dot(a, b, ca=1, cb=0):
    return lax.dot_general(a, b, (((ca,), (cb,)), ((), ())), preferred_element_type=F32)


def selections():
    first = np.zeros((288, 288), np.float32)
    second = np.zeros((2, 144, 144), np.float32)
    gather = np.zeros((3, 288, 144), np.float32)
    leave = np.zeros((160, 144), np.float32)
    place = np.zeros((4, T, 40), np.float32)
    for p in range(2):
        for a in range(6):
            for b in range(12):
                slab = (a * 12 + b) * 2 + (p + 1) % 2
                half = (p * 6 + a) * 6 + b % 6
                wide = (p * 3 + a % 3) * 12 + (b + 6) % 12
                for arr in range(2):
                    first[(0 if b < 6 else 144) + arr * 72 + half, arr * T + slab] = 1
                    source = 1 if b < 6 else 0
                    if a < 3:
                        second[source, arr * 72 + wide, arr * 72 + half] = 1
                    else:
                        token = (p * 6 + a - 3) * 12 + (b + 6) % 12
                        gather[source, arr * 144 + token, arr * 72 + half] = 1
                token = (p * 6 + a) * 12 + b
                if a >= 3:
                    for arr in range(2):
                        row = (p * 3 + a - 3) * 12 + b
                        gather[2, arr * 144 + token, arr * 72 + row] = 1
                row = (p * 3 + a % 3) * 6 + b % 6
                leave[(80 if a >= 3 else 0) + (40 if b >= 6 else 0) + row, token] = 1
                home = (((a + 3) % 6) * 12 + (b + 6) % 12) * 2 + (p + 1) % 2
                place[(2 if b >= 6 else 0) + (1 if a >= 3 else 0), home, row] = 1
    return [jnp.asarray(m, BF16) for m in (first, second, gather, leave, place)]


def pack_kernel(tok, cot, sel, idx, strip, kept, packed, tok_in, cot_in, sel_in, idx_in, rows, sems):
    copies = [
        pltpu.make_async_copy(src, dst, sems.at[k])
        for k, (src, dst) in enumerate(
            ((tok, tok_in), (cot, cot_in), (sel, sel_in), (idx, idx_in))
        )
    ]
    for copy in copies:
        copy.start()
    for arr, ref in enumerate((tok_in, cot_in)):
        copies[arr].wait()
        for k in range(72):
            at = arr * T + 2 * k
            rows[at : at + 2, :] = ref[k // 12, k % 12].astype(F32)
    copies[2].wait()
    out = dot(sel_in[...], rows[...].astype(BF16)).astype(BF16)
    strip[...] = out[0:T]
    kept[...] = out[T:]
    copies[3].wait()
    packed[0:T, :] = idx_in[:, 0:128]
    packed[T:PACK, :] = packed_rows(idx_in)


def repack_kernel(kept, arrived, sel, strip):
    strip[...] = (dot(sel[0], kept[...]) + dot(sel[1], arrived[...])).astype(BF16)


def unpack_kernel(kept, first, second, sel, out, rows):
    total = dot(sel[0], kept[0]) + dot(sel[1], first[0])
    rows[...] = total + dot(sel[2], second[0]) + dot(sel[3], second[1])
    for k in range(72):
        out[k // 12, k % 12] = rows[2 * k : 2 * k + 2, :].astype(BF16)


def mix_kernel(parts, scattered, out, wide):
    n, rows, _ = out.shape
    bias_rows = scattered.shape[0] // n
    rows = rows - bias_rows
    wide[...] = jnp.sum(parts[...].astype(F32), axis=0)
    for k in range(n):
        mine = wide[rows * k : rows * k + rows, :]
        theirs = scattered[bias_rows * k : bias_rows * k + bias_rows, :]
        out[k] = jnp.concatenate((mine, theirs), axis=0).astype(BF16)


def sum_kernel(parts, out):
    total = jnp.sum(parts[...].astype(F32), axis=0).astype(BF16)
    for k in range(out.shape[0]):
        out[k] = total


def split_kernel(parts, out, scattered, wide):
    n = parts.shape[0]
    bias_rows = scattered.shape[0] // n
    rows = parts.shape[1] - bias_rows
    for k in range(n):
        part = parts[k].astype(F32)
        wide[rows * k : rows * k + rows, :] = part[0:rows]
        scattered[bias_rows * k : bias_rows * k + bias_rows, :] = part[rows:]
    total = wide[...].astype(BF16)
    for k in range(out.shape[0]):
        out[k] = total


def finish_kernel(parts, qkv, proj):
    wide = parts[...].reshape(6 * C, 128).astype(F32)
    for k in range(4):
        qkv[:, 128 * k : 128 * k + 128] = wide[C * k : C * k + C]
    qkv[:, 512:576] = wide[4 * C : 5 * C, 0:64]
    proj[:, 0:64] = wide[4 * C : 5 * C, 64:128]
    proj[:, 64:C] = wide[5 * C : 6 * C]


def packed_rows(idx):
    lane = lax.broadcasted_iota(jnp.int32, (24, 128), 1)
    tail = jnp.zeros((24, 128), jnp.int32)
    for c in range(6):
        part = jnp.concatenate(
            (idx[24 * c : 24 * c + 24, 128:T], jnp.zeros((24, 112), jnp.int32)), axis=1
        )
        part = pltpu.roll(part, 16 * c, 1) if c else part
        tail = jnp.where((lane >= 16 * c) & (lane < 16 * c + 16), part, tail)
    return tail


def bias_body(first, table, col, row, packed, bias, flat):
    def block(i, carry):
        at = pl.ds(pl.multiple_of(i * 8, 8), 8)
        position = packed[at, :]
        low = position & 127
        high = position >> 7
        totals = [jnp.zeros((8, 128), F32)] * HALF
        for k in range(BLKS):
            here = high == k
            for h in range(HALF):
                r = (first + h) * BLKS + k
                values = jnp.broadcast_to(table[r : r + 1, :], (8, 128))
                found = jnp.take_along_axis(values, low, axis=1, mode="promise_in_bounds")
                totals[h] = jnp.where(here, found, totals[h])
        for h in range(HALF):
            flat[h, at, :] = totals[h]
        return carry

    lax.fori_loop(0, PACK // 8, block, 0)
    same = col[...] == row[...]
    for h in range(HALF):
        bias[h, :, 0:128] = jnp.where(same[:, 0:128], flat[h, 0:T, :], -1e9)
        tail = flat[h, T:PACK, :]
        for c in range(6):
            part = pltpu.roll(tail, 128 - 16 * c, 1) if c else tail
            at = slice(24 * c, 24 * c + 24)
            bias[h, at, 128:T] = jnp.where(same[at, 128:T], part[:, 0:16], -1e9)


def bias_first_kernel(packed, table, col, row, bias, flat):
    bias_body(0, table, col, row, packed, bias, flat)


def bias_second_kernel(packed, table, col, row, bias, flat):
    bias_body(HALF, table, col, row, packed, bias, flat)


def main_kernel(kept, lon, lat, sel, bias_a, bias_b, wqkv, wproj,
                grads, ds_out, grad_in_out, normed_out, inv_std_out, cot_out, ds_tail):
    scale = HD ** (-0.5)
    both = dot(sel[0], kept[...]) + dot(sel[1], lon[...]) + dot(sel[2], lat[...])
    values = both[0:T]
    cot = both[T:].astype(BF16)
    center = values - jnp.mean(values, axis=-1, keepdims=True)
    inv_std = lax.rsqrt(jnp.mean(center * center, axis=-1, keepdims=True) + 1e-05)
    normed = center * inv_std
    hidden = normed.astype(BF16)
    proj = dot(hidden, wqkv[...])
    query = proj[:, 0:C]
    query_t = query.T.astype(BF16)
    query = query.astype(BF16)
    key = proj[:, C : 2 * C].astype(BF16)
    value = proj[:, 2 * C :].astype(BF16)
    att = dot(cot, wproj[...], 1, 1)
    att_t = att.T.astype(BF16)
    att = att.astype(BF16)
    head = lax.broadcasted_iota(jnp.int32, (T, C), 1) // HD
    zero = jnp.zeros((T, C), BF16)
    attended = jnp.zeros((T, C), F32)
    grad_query = jnp.zeros((T, C), F32)
    key_t = []
    value_t = []
    lane = lax.broadcasted_iota(jnp.int32, (24, 128), 1)
    for h in range(HEADS):
        mine = head == h
        scores = dot(jnp.where(mine, query, zero), key, 1, 1) * scale
        scores = scores + (bias_a[h] if h < HALF else bias_b[h - HALF])
        exponent = jnp.exp(scores - jnp.max(scores, axis=-1, keepdims=True))
        prob = exponent * (1.0 / jnp.sum(exponent, axis=-1, keepdims=True))
        prob_half = prob.astype(BF16)
        attended = attended + dot(prob_half, jnp.where(mine, value, zero))
        grad_prob = dot(jnp.where(mine, att, zero), value, 1, 1)
        value_t.append(dot(att_t[HD * h : HD * h + HD], prob_half))
        ds = prob * (grad_prob - jnp.sum(grad_prob * prob, axis=-1, keepdims=True))
        ds_half = ds.astype(BF16)
        grad_query = grad_query + dot(ds_half, jnp.where(mine, key, zero))
        key_t.append(dot(query_t[HD * h : HD * h + HD], ds_half))
        ds_out[h, 0:T, :] = ds[:, 0:128]
        ds_tail[:, 0:16] = ds[:, 128:T]
        packed = jnp.zeros((24, 128), F32)
        for c in range(6):
            part = ds_tail[24 * c : 24 * c + 24, :]
            part = pltpu.roll(part, 16 * c, 1) if c else part
            packed = jnp.where((lane >= 16 * c) & (lane < 16 * c + 16), part, packed)
        ds_out[h, T:PACK, :] = packed
    grad_key = jnp.concatenate(key_t, axis=0).T
    grad_value = jnp.concatenate(value_t, axis=0).T
    grad_in = jnp.concatenate((grad_query * scale, grad_key * scale, grad_value), axis=1)
    grad_in = grad_in.astype(BF16)
    grad_qkv = dot(hidden, grad_in, 0, 0)
    grad_proj = dot(attended.astype(BF16), cot, 0, 0)
    both = jnp.concatenate((grad_qkv, grad_proj), axis=1).astype(BF16)
    for k in range(6):
        grads[C * k : C * k + C, :] = both[:, 128 * k : 128 * k + 128]
    grad_in_out[...] = grad_in
    normed_out[...] = normed
    inv_std_out[...] = inv_std
    cot_out[...] = cot


def norm_kernel(grad_in, normed_ref, inv_std, cot, wqkv, leave, ret_kept, ret_strip):
    normed = normed_ref[...]
    grad_hidden = dot(grad_in[...], wqkv[...], 1, 1)
    grad_norm = inv_std[...] * (
        grad_hidden
        - jnp.mean(grad_hidden, axis=-1, keepdims=True)
        - normed * jnp.mean(grad_hidden * normed, axis=-1, keepdims=True)
    )
    returned = (cot[...].astype(F32) + grad_norm).astype(BF16)
    parts = dot(leave[...], returned).astype(BF16)
    for k in range(2):
        ret_kept[k] = parts[40 * k : 40 * k + 40]
        ret_strip[k] = parts[80 + 40 * k : 120 + 40 * k]


def scatter_kernel(packed, ds, out, total):
    total[...] = jnp.zeros_like(total)
    blocks = lax.broadcasted_iota(jnp.int32, (32, 128), 0)
    lows = lax.broadcasted_iota(jnp.int32, (128, 128), 0)

    def block(i, carry):
        at = pl.ds(pl.multiple_of(i * 8, 8), 8)
        position = packed[at, :]
        low = position & 127
        high = position >> 7
        left = []
        right = []
        for r in range(8):
            right.append(jnp.where(lows == low[r : r + 1], 1.0, 0.0).astype(BF16))
            mine = blocks == high[r : r + 1]
            parts = []
            for h in range(HEADS):
                row = ds[h, at, :][r : r + 1]
                parts.append(jnp.where(mine, row, 0.0).astype(BF16))
            left.append(jnp.concatenate(parts, axis=0))
        total[...] += dot(jnp.concatenate(left, axis=1), jnp.concatenate(right, axis=1), 1, 1)
        return carry

    lax.fori_loop(0, PACK // 8, block, 0)
    out[...] = total[...]


def call(kernel, shapes, scratch, cost, *args, copies=0):
    scratch = [pltpu.VMEM(s, d) for s, d in scratch]
    specs = {}
    if copies:
        scratch.append(pltpu.SemaphoreType.DMA((copies,)))
        specs["in_specs"] = [pl.BlockSpec(memory_space=pltpu.MemorySpace.HBM)] * copies
    return pl.pallas_call(
        kernel,
        out_shape=[jax.ShapeDtypeStruct(s, d) for s, d in shapes],
        scratch_shapes=scratch,
        compiler_params=pltpu.CompilerParams(vmem_limit_bytes=(56 if copies else 48) << 20),
        cost_estimate=pl.CostEstimate(flops=cost, bytes_accessed=1 << 20, transcendentals=0),
        **specs,
    )(*args)


def exchange(block, axes, groups=None):
    return lax.all_to_all(block, axes, 0, 0, axis_index_groups=groups, tiled=False)


def local(sizes, tokens, cotangent, region, pos_index, w_qkv, w_proj, bias_table):
    n_lon, n_lat, n_y = sizes
    n_z = n_lon // n_y
    first, second, gather, leave, place = selections()
    across = ("lat", "rep")

    def moved(block, axes, n, distance):
        return lax.ppermute(block, axes, [((i + distance) % n, i) for i in range(n)])

    table = jnp.pad(bias_table.reshape(ROWS, HEADS).T, ((0, 0), (0, BLKS * 128 - ROWS)))
    table = table.reshape(HEADS * BLKS, 128)

    col, row = region.reshape(T, 1), region.reshape(1, T)
    bias_shape = ((HALF, T, T), F32)
    bias_scratch = [((HALF, PACK, 128), F32)]
    block = ((T, C), BF16)
    order = (1, 2, 0, 3)
    stored = ((6, 12, 2, C), BF16)
    strip, kept, packed = call(
        pack_kernel,
        [block] * 2 + [((PACK, 128), jnp.int32)],
        [stored, stored, ((2 * T, 2 * T), BF16), ((T, T), jnp.int32), ((2 * T, C), F32)],
        10**8,
        tokens.transpose(order), cotangent.transpose(order), first, pos_index,
        copies=4,
    )
    lon = moved(strip, "lon", n_lon, 1)
    (bias_a,) = call(
        bias_first_kernel, [bias_shape], bias_scratch, 3 * 10**9, packed, table, col, row
    )
    (strip,) = call(repack_kernel, [block], [], 10**8, kept, lon, second)
    strip, late_packed = lax.optimization_barrier((strip, packed))
    lat = moved(strip, across, n_lat, 1)
    (bias_b,) = call(
        bias_second_kernel, [bias_shape], bias_scratch, 3 * 10**9, late_packed, table, col, row
    )
    grads, ds, grad_in, normed, inv_std, cot = call(
        main_kernel,
        [
            ((6 * C, 128), BF16),
            ((HEADS, PACK, 128), F32),
            ((T, 3 * C), BF16),
            ((T, C), F32),
            ((T, 1), F32),
            block,
        ],
        [((T, 128), F32)],
        10**10,
        kept, lon, lat, gather, bias_a, bias_b, w_qkv, w_proj,
    )
    rows_y = [[z * n_y + y for y in range(n_y)] for z in range(n_z)]
    rows_z = [[z * n_y + y for z in range(n_z)] for y in range(n_y)]
    rows = 6 * C // n_lat
    grads = exchange(grads.reshape(n_lat, rows, 128), across)
    (scattered,) = call(
        scatter_kernel, [((192, 128), F32)], [((192, 128), F32)], 5 * 10**9, packed, ds
    )
    mixed_rows = (rows + 192) // n_y
    wide = [((rows, 128), F32)]
    (mixed,) = call(
        mix_kernel, [((n_y, mixed_rows, 128), BF16)], wide, 10**7, grads, scattered
    )
    mixed, grad_in = lax.optimization_barrier((mixed, grad_in))
    quarter = ((2, 40, C), BF16)
    ret_kept, ret_strip = call(
        norm_kernel, [quarter] * 2, [], 10**8, grad_in, normed, inv_std, cot, w_qkv, leave
    )
    ret_first = moved(ret_strip, across, n_lat, -1)
    mixed = exchange(mixed, "lon", rows_y)
    (mixed,) = call(sum_kernel, [((n_z, mixed_rows, 128), BF16)], [], 10**7, mixed)
    mixed = exchange(mixed, "lon", rows_z)
    (mixed,) = call(sum_kernel, [((n_y, mixed_rows, 128), BF16)], [], 10**7, mixed)
    mixed, ret_first = lax.optimization_barrier((mixed, ret_first))
    ret_second = moved(jnp.stack((ret_kept[1], ret_first[1])), "lon", n_lon, -1)
    mixed = exchange(mixed, "lon", rows_y)
    grads, scattered = call(
        split_kernel, [((n_lat, rows, 128), BF16), ((192, 128), F32)], wide, 10**7, mixed
    )
    grads, ret_second = lax.optimization_barrier((grads, ret_second))
    grads = exchange(grads, across)
    (grad_tokens,) = call(
        unpack_kernel, [((6, 12, 2, C), BF16)], [((T, C), F32)], 10**8,
        ret_kept, ret_first, ret_second, place,
    )
    scattered = scattered.reshape(HEADS, 32 * 128)
    grad_bias = scattered[:, :ROWS].T.reshape(ROWS, 1, HEADS)
    grad_qkv, grad_proj = call(
        finish_kernel, [((C, 3 * C), F32), ((C, C), F32)], [], 10**7, grads
    )
    return (grad_tokens.transpose(2, 0, 1, 3), grad_qkv, grad_proj, grad_bias)


def solution(mesh):
    n_lon = mesh.shape["lon"]
    n_lat = mesh.shape["lat"] * mesh.shape["rep"]
    n_y = 8 if n_lon % 8 == 0 else 2
    placed = (
        P(None, ("lat", "rep"), "lon", None),
        P(None, ("lat", "rep"), "lon", None),
        P(None, ("lat", "rep"), "lon"),
        P(),
        P(),
        P(),
        P(None, ("lat", "rep"), None),
    )
    return jax.shard_map(
        functools.partial(local, (n_lon, n_lat, n_y)),
        mesh=mesh,
        in_specs=placed,
        out_specs=(P(None, ("lat", "rep"), "lon", None), P(), P(), P(None, ("lat", "rep"), None)),
        check_vma=False,
    )
```

```python
import functools

import jax
import jax.numpy as jnp
import numpy as np
from jax import lax
from jax.experimental import pallas as pl
from jax.experimental.pallas import tpu as pltpu
from jax.sharding import PartitionSpec as P

F32 = jnp.float32
BF16 = jnp.bfloat16
T = 144
C = 192
HEADS = 6
HD = 32
ROWS = 3312
BLKS = 26
PACK = 168
HALF = HEADS // 2


def dot(a, b, ca=1, cb=0):
    return lax.dot_general(a, b, (((ca,), (cb,)), ((), ())), preferred_element_type=F32)


def selections():
    first = np.zeros((288, 288), np.float32)
    second = np.zeros((2, 144, 144), np.float32)
    gather = np.zeros((3, 288, 144), np.float32)
    leave = np.zeros((160, 144), np.float32)
    place = np.zeros((4, T, 40), np.float32)
    for p in range(2):
        for a in range(6):
            for b in range(12):
                slab = (a * 12 + b) * 2 + (p + 1) % 2
                half = (p * 6 + a) * 6 + b % 6
                wide = (p * 3 + a % 3) * 12 + (b + 6) % 12
                for arr in range(2):
                    first[(0 if b < 6 else 144) + arr * 72 + half, arr * T + slab] = 1
                    source = 1 if b < 6 else 0
                    if a < 3:
                        second[source, arr * 72 + wide, arr * 72 + half] = 1
                    else:
                        token = (p * 6 + a - 3) * 12 + (b + 6) % 12
                        gather[source, arr * 144 + token, arr * 72 + half] = 1
                token = (p * 6 + a) * 12 + b
                if a >= 3:
                    for arr in range(2):
                        row = (p * 3 + a - 3) * 12 + b
                        gather[2, arr * 144 + token, arr * 72 + row] = 1
                row = (p * 3 + a % 3) * 6 + b % 6
                leave[(80 if a >= 3 else 0) + (40 if b >= 6 else 0) + row, token] = 1
                home = (((a + 3) % 6) * 12 + (b + 6) % 12) * 2 + (p + 1) % 2
                place[(2 if b >= 6 else 0) + (1 if a >= 3 else 0), home, row] = 1
    return [jnp.asarray(m, BF16) for m in (first, second, gather, leave, place)]


def pack_kernel(tok, cot, sel, idx, strip, kept, packed, tok_in, cot_in, sel_in, idx_in, rows, sems):
    copies = [
        pltpu.make_async_copy(src, dst, sems.at[k])
        for k, (src, dst) in enumerate(
            ((tok, tok_in), (cot, cot_in), (sel, sel_in), (idx, idx_in))
        )
    ]
    for copy in copies:
        copy.start()
    for arr, ref in enumerate((tok_in, cot_in)):
        copies[arr].wait()
        for k in range(72):
            at = arr * T + 2 * k
            rows[at : at + 2, :] = ref[k // 12, k % 12].astype(F32)
    copies[2].wait()
    out = dot(sel_in[...], rows[...].astype(BF16)).astype(BF16)
    strip[...] = out[0:T]
    kept[...] = out[T:]
    copies[3].wait()
    packed[0:T, :] = idx_in[:, 0:128]
    packed[T:PACK, :] = packed_rows(idx_in)


def repack_kernel(kept, arrived, sel, strip):
    strip[...] = (dot(sel[0], kept[...]) + dot(sel[1], arrived[...])).astype(BF16)


def unpack_kernel(kept, first, second, sel, out, rows):
    total = dot(sel[0], kept[0]) + dot(sel[1], first[0])
    rows[...] = total + dot(sel[2], second[0]) + dot(sel[3], second[1])
    for k in range(72):
        out[k // 12, k % 12] = rows[2 * k : 2 * k + 2, :].astype(BF16)


def mix_kernel(parts, scattered, out, wide):
    n, rows, _ = out.shape
    bias_rows = scattered.shape[0] // n
    rows = rows - bias_rows
    wide[...] = jnp.sum(parts[...].astype(F32), axis=0)
    for k in range(n):
        mine = wide[rows * k : rows * k + rows, :]
        theirs = scattered[bias_rows * k : bias_rows * k + bias_rows, :]
        out[k] = jnp.concatenate((mine, theirs), axis=0).astype(BF16)


def sum_kernel(parts, out):
    total = jnp.sum(parts[...].astype(F32), axis=0).astype(BF16)
    for k in range(out.shape[0]):
        out[k] = total


def split_kernel(parts, out, scattered, wide):
    n = parts.shape[0]
    bias_rows = scattered.shape[0] // n
    rows = parts.shape[1] - bias_rows
    for k in range(n):
        part = parts[k].astype(F32)
        wide[rows * k : rows * k + rows, :] = part[0:rows]
        scattered[bias_rows * k : bias_rows * k + bias_rows, :] = part[rows:]
    total = wide[...].astype(BF16)
    for k in range(out.shape[0]):
        out[k] = total


def finish_kernel(parts, qkv, proj):
    wide = parts[...].reshape(6 * C, 128).astype(F32)
    for k in range(4):
        qkv[:, 128 * k : 128 * k + 128] = wide[C * k : C * k + C]
    qkv[:, 512:576] = wide[4 * C : 5 * C, 0:64]
    proj[:, 0:64] = wide[4 * C : 5 * C, 64:128]
    proj[:, 64:C] = wide[5 * C : 6 * C]


def packed_rows(idx):
    lane = lax.broadcasted_iota(jnp.int32, (24, 128), 1)
    tail = jnp.zeros((24, 128), jnp.int32)
    for c in range(6):
        part = jnp.concatenate(
            (idx[24 * c : 24 * c + 24, 128:T], jnp.zeros((24, 112), jnp.int32)), axis=1
        )
        part = pltpu.roll(part, 16 * c, 1) if c else part
        tail = jnp.where((lane >= 16 * c) & (lane < 16 * c + 16), part, tail)
    return tail


def bias_body(first, table, col, row, packed, bias, flat):
    def block(i, carry):
        at = pl.ds(pl.multiple_of(i * 8, 8), 8)
        position = packed[at, :]
        low = position & 127
        high = position >> 7
        totals = [jnp.zeros((8, 128), F32)] * HALF
        for k in range(BLKS):
            here = high == k
            for h in range(HALF):
                r = (first + h) * BLKS + k
                values = jnp.broadcast_to(table[r : r + 1, :], (8, 128))
                found = jnp.take_along_axis(values, low, axis=1, mode="promise_in_bounds")
                totals[h] = jnp.where(here, found, totals[h])
        for h in range(HALF):
            flat[h, at, :] = totals[h]
        return carry

    lax.fori_loop(0, PACK // 8, block, 0)
    same = col[...] == row[...]
    for h in range(HALF):
        bias[h, :, 0:128] = jnp.where(same[:, 0:128], flat[h, 0:T, :], -1e9)
        tail = flat[h, T:PACK, :]
        for c in range(6):
            part = pltpu.roll(tail, 128 - 16 * c, 1) if c else tail
            at = slice(24 * c, 24 * c + 24)
            bias[h, at, 128:T] = jnp.where(same[at, 128:T], part[:, 0:16], -1e9)


def bias_first_kernel(packed, table, col, row, bias, flat):
    bias_body(0, table, col, row, packed, bias, flat)


def bias_second_kernel(packed, table, col, row, bias, flat):
    bias_body(HALF, table, col, row, packed, bias, flat)


def main_kernel(kept, lon, lat, sel, bias_a, bias_b, wqkv, wproj,
                grads, ds_out, grad_in_out, normed_out, inv_std_out, cot_out, ds_tail):
    scale = HD ** (-0.5)
    both = dot(sel[0], kept[...]) + dot(sel[1], lon[...]) + dot(sel[2], lat[...])
    values = both[0:T]
    cot = both[T:].astype(BF16)
    center = values - jnp.mean(values, axis=-1, keepdims=True)
    inv_std = lax.rsqrt(jnp.mean(center * center, axis=-1, keepdims=True) + 1e-05)
    normed = center * inv_std
    hidden = normed.astype(BF16)
    proj = dot(hidden, wqkv[...])
    query = proj[:, 0:C]
    query_t = query.T.astype(BF16)
    query = query.astype(BF16)
    key = proj[:, C : 2 * C].astype(BF16)
    value = proj[:, 2 * C :].astype(BF16)
    att = dot(cot, wproj[...], 1, 1)
    att_t = att.T.astype(BF16)
    att = att.astype(BF16)
    head = lax.broadcasted_iota(jnp.int32, (T, C), 1) // HD
    zero = jnp.zeros((T, C), BF16)
    attended = jnp.zeros((T, C), F32)
    grad_query = jnp.zeros((T, C), F32)
    key_t = []
    value_t = []
    lane = lax.broadcasted_iota(jnp.int32, (24, 128), 1)
    for h in range(HEADS):
        mine = head == h
        scores = dot(jnp.where(mine, query, zero), key, 1, 1) * scale
        scores = scores + (bias_a[h] if h < HALF else bias_b[h - HALF])
        exponent = jnp.exp(scores - jnp.max(scores, axis=-1, keepdims=True))
        prob = exponent * (1.0 / jnp.sum(exponent, axis=-1, keepdims=True))
        prob_half = prob.astype(BF16)
        attended = attended + dot(prob_half, jnp.where(mine, value, zero))
        grad_prob = dot(jnp.where(mine, att, zero), value, 1, 1)
        value_t.append(dot(att_t[HD * h : HD * h + HD], prob_half))
        ds = prob * (grad_prob - jnp.sum(grad_prob * prob, axis=-1, keepdims=True))
        ds_half = ds.astype(BF16)
        grad_query = grad_query + dot(ds_half, jnp.where(mine, key, zero))
        key_t.append(dot(query_t[HD * h : HD * h + HD], ds_half))
        ds_out[h, 0:T, :] = ds[:, 0:128]
        ds_tail[:, 0:16] = ds[:, 128:T]
        packed = jnp.zeros((24, 128), F32)
        for c in range(6):
            part = ds_tail[24 * c : 24 * c + 24, :]
            part = pltpu.roll(part, 16 * c, 1) if c else part
            packed = jnp.where((lane >= 16 * c) & (lane < 16 * c + 16), part, packed)
        ds_out[h, T:PACK, :] = packed
    grad_key = jnp.concatenate(key_t, axis=0).T
    grad_value = jnp.concatenate(value_t, axis=0).T
    grad_in = jnp.concatenate((grad_query * scale, grad_key * scale, grad_value), axis=1)
    grad_in = grad_in.astype(BF16)
    grad_qkv = dot(hidden, grad_in, 0, 0)
    grad_proj = dot(attended.astype(BF16), cot, 0, 0)
    both = jnp.concatenate((grad_qkv, grad_proj), axis=1).astype(BF16)
    for k in range(6):
        grads[C * k : C * k + C, :] = both[:, 128 * k : 128 * k + 128]
    grad_in_out[...] = grad_in
    normed_out[...] = normed
    inv_std_out[...] = inv_std
    cot_out[...] = cot


def norm_kernel(grad_in, normed_ref, inv_std, cot, wqkv, leave, ret_kept, ret_strip):
    normed = normed_ref[...]
    grad_hidden = dot(grad_in[...], wqkv[...], 1, 1)
    grad_norm = inv_std[...] * (
        grad_hidden
        - jnp.mean(grad_hidden, axis=-1, keepdims=True)
        - normed * jnp.mean(grad_hidden * normed, axis=-1, keepdims=True)
    )
    returned = (cot[...].astype(F32) + grad_norm).astype(BF16)
    parts = dot(leave[...], returned).astype(BF16)
    for k in range(2):
        ret_kept[k] = parts[40 * k : 40 * k + 40]
        ret_strip[k] = parts[80 + 40 * k : 120 + 40 * k]


def scatter_kernel(packed, ds, out, total):
    total[...] = jnp.zeros_like(total)
    blocks = lax.broadcasted_iota(jnp.int32, (32, 128), 0)
    lows = lax.broadcasted_iota(jnp.int32, (128, 128), 0)

    def block(i, carry):
        at = pl.ds(pl.multiple_of(i * 8, 8), 8)
        position = packed[at, :]
        low = position & 127
        high = position >> 7
        left = []
        right = []
        for r in range(8):
            right.append(jnp.where(lows == low[r : r + 1], 1.0, 0.0).astype(BF16))
            mine = blocks == high[r : r + 1]
            parts = []
            for h in range(HEADS):
                row = ds[h, at, :][r : r + 1]
                parts.append(jnp.where(mine, row, 0.0).astype(BF16))
            left.append(jnp.concatenate(parts, axis=0))
        total[...] += dot(jnp.concatenate(left, axis=1), jnp.concatenate(right, axis=1), 1, 1)
        return carry

    lax.fori_loop(0, PACK // 8, block, 0)
    out[...] = total[...]


def call(kernel, shapes, scratch, cost, *args, copies=0):
    scratch = [pltpu.VMEM(s, d) for s, d in scratch]
    specs = {}
    if copies:
        scratch.append(pltpu.SemaphoreType.DMA((copies,)))
        specs["in_specs"] = [pl.BlockSpec(memory_space=pltpu.MemorySpace.HBM)] * copies
    if copies:
        args = [pltpu.with_memory_space_constraint(a, pltpu.MemorySpace.HBM) for a in args]
    return pl.pallas_call(
        kernel,
        out_shape=[jax.ShapeDtypeStruct(s, d) for s, d in shapes],
        scratch_shapes=scratch,
        compiler_params=pltpu.CompilerParams(vmem_limit_bytes=(48 if copies else 48) << 20),
        cost_estimate=pl.CostEstimate(flops=cost, bytes_accessed=1 << 20, transcendentals=0),
        **specs,
    )(*args)


def exchange(block, axes, groups=None):
    return lax.all_to_all(block, axes, 0, 0, axis_index_groups=groups, tiled=False)


def local(sizes, tokens, cotangent, region, pos_index, w_qkv, w_proj, bias_table):
    n_lon, n_lat, n_y = sizes
    n_z = n_lon // n_y
    first, second, gather, leave, place = selections()
    across = ("lat", "rep")

    def moved(block, axes, n, distance):
        return lax.ppermute(block, axes, [((i + distance) % n, i) for i in range(n)])

    table = jnp.pad(bias_table.reshape(ROWS, HEADS).T, ((0, 0), (0, BLKS * 128 - ROWS)))
    table = table.reshape(HEADS * BLKS, 128)

    col, row = region.reshape(T, 1), region.reshape(1, T)
    bias_shape = ((HALF, T, T), F32)
    bias_scratch = [((HALF, PACK, 128), F32)]
    block = ((T, C), BF16)
    order = (1, 2, 0, 3)
    stored = ((6, 12, 2, C), BF16)
    strip, kept, packed = call(
        pack_kernel,
        [block] * 2 + [((PACK, 128), jnp.int32)],
        [stored, stored, ((2 * T, 2 * T), BF16), ((T, T), jnp.int32), ((2 * T, C), F32)],
        10**8,
        tokens.transpose(order), cotangent.transpose(order), first, pos_index,
        copies=4,
    )
    lon = moved(strip, "lon", n_lon, 1)
    (bias_a,) = call(
        bias_first_kernel, [bias_shape], bias_scratch, 3 * 10**9, packed, table, col, row
    )
    (strip,) = call(repack_kernel, [block], [], 10**8, kept, lon, second)
    strip, late_packed = lax.optimization_barrier((strip, packed))
    lat = moved(strip, across, n_lat, 1)
    (bias_b,) = call(
        bias_second_kernel, [bias_shape], bias_scratch, 3 * 10**9, late_packed, table, col, row
    )
    grads, ds, grad_in, normed, inv_std, cot = call(
        main_kernel,
        [
            ((6 * C, 128), BF16),
            ((HEADS, PACK, 128), F32),
            ((T, 3 * C), BF16),
            ((T, C), F32),
            ((T, 1), F32),
            block,
        ],
        [((T, 128), F32)],
        10**10,
        kept, lon, lat, gather, bias_a, bias_b, w_qkv, w_proj,
    )
    rows_y = [[z * n_y + y for y in range(n_y)] for z in range(n_z)]
    rows_z = [[z * n_y + y for z in range(n_z)] for y in range(n_y)]
    rows = 6 * C // n_lat
    grads = exchange(grads.reshape(n_lat, rows, 128), across)
    (scattered,) = call(
        scatter_kernel, [((192, 128), F32)], [((192, 128), F32)], 5 * 10**9, packed, ds
    )
    mixed_rows = (rows + 192) // n_y
    wide = [((rows, 128), F32)]
    (mixed,) = call(
        mix_kernel, [((n_y, mixed_rows, 128), BF16)], wide, 10**7, grads, scattered
    )
    mixed = exchange(mixed, "lon", rows_y)
    (mixed,) = call(sum_kernel, [((n_z, mixed_rows, 128), BF16)], [], 10**7, mixed)
    mixed = exchange(mixed, "lon", rows_z)
    (mixed,) = call(sum_kernel, [((n_y, mixed_rows, 128), BF16)], [], 10**7, mixed)
    mixed, grad_in = lax.optimization_barrier((mixed, grad_in))
    quarter = ((2, 40, C), BF16)
    ret_kept, ret_strip = call(
        norm_kernel, [quarter] * 2, [], 10**8, grad_in, normed, inv_std, cot, w_qkv, leave
    )
    ret_first = moved(ret_strip, across, n_lat, -1)
    mixed = exchange(mixed, "lon", rows_y)
    grads, scattered = call(
        split_kernel, [((n_lat, rows, 128), BF16), ((192, 128), F32)], wide, 10**7, mixed
    )
    grads, ret_first = lax.optimization_barrier((grads, ret_first))
    ret_second = moved(jnp.stack((ret_kept[1], ret_first[1])), "lon", n_lon, -1)
    grads = exchange(grads, across)
    (grad_tokens,) = call(
        unpack_kernel, [((6, 12, 2, C), BF16)], [((T, C), F32)], 10**8,
        ret_kept, ret_first, ret_second, place,
    )
    scattered = scattered.reshape(HEADS, 32 * 128)
    grad_bias = scattered[:, :ROWS].T.reshape(ROWS, 1, HEADS)
    grad_qkv, grad_proj = call(
        finish_kernel, [((C, 3 * C), F32), ((C, C), F32)], [], 10**7, grads
    )
    return (grad_tokens.transpose(2, 0, 1, 3), grad_qkv, grad_proj, grad_bias)


def solution(mesh):
    n_lon = mesh.shape["lon"]
    n_lat = mesh.shape["lat"] * mesh.shape["rep"]
    n_y = 8 if n_lon % 8 == 0 else 2
    placed = (
        P(None, ("lat", "rep"), "lon", None),
        P(None, ("lat", "rep"), "lon", None),
        P(None, ("lat", "rep"), "lon"),
        P(),
        P(),
        P(),
        P(None, ("lat", "rep"), None),
    )
    return jax.shard_map(
        functools.partial(local, (n_lon, n_lat, n_y)),
        mesh=mesh,
        in_specs=placed,
        out_specs=(P(None, ("lat", "rep"), "lon", None), P(), P(), P(None, ("lat", "rep"), None)),
        check_vma=False,
    )
```

```python
import functools

import jax
import jax.numpy as jnp
import numpy as np
from jax import lax
from jax.experimental import pallas as pl
from jax.experimental.pallas import tpu as pltpu
from jax.sharding import PartitionSpec as P

F32 = jnp.float32
BF16 = jnp.bfloat16
T = 144
C = 192
HEADS = 6
HD = 32
ROWS = 3312
BLKS = 26
PACK = 168
HALF = HEADS // 2


def dot(a, b, ca=1, cb=0):
    return lax.dot_general(a, b, (((ca,), (cb,)), ((), ())), preferred_element_type=F32)


def selections():
    first = np.zeros((288, 288), np.float32)
    second = np.zeros((2, 144, 144), np.float32)
    gather = np.zeros((3, 288, 144), np.float32)
    leave = np.zeros((160, 144), np.float32)
    place = np.zeros((4, T, 40), np.float32)
    for p in range(2):
        for a in range(6):
            for b in range(12):
                slab = (a * 12 + b) * 2 + (p + 1) % 2
                half = (p * 6 + a) * 6 + b % 6
                wide = (p * 3 + a % 3) * 12 + (b + 6) % 12
                for arr in range(2):
                    first[(0 if b < 6 else 144) + arr * 72 + half, arr * T + slab] = 1
                    source = 1 if b < 6 else 0
                    if a < 3:
                        second[source, arr * 72 + wide, arr * 72 + half] = 1
                    else:
                        token = (p * 6 + a - 3) * 12 + (b + 6) % 12
                        gather[source, arr * 144 + token, arr * 72 + half] = 1
                token = (p * 6 + a) * 12 + b
                if a >= 3:
                    for arr in range(2):
                        row = (p * 3 + a - 3) * 12 + b
                        gather[2, arr * 144 + token, arr * 72 + row] = 1
                row = (p * 3 + a % 3) * 6 + b % 6
                leave[(80 if a >= 3 else 0) + (40 if b >= 6 else 0) + row, token] = 1
                home = (((a + 3) % 6) * 12 + (b + 6) % 12) * 2 + (p + 1) % 2
                place[(2 if b >= 6 else 0) + (1 if a >= 3 else 0), home, row] = 1
    return [jnp.asarray(m, BF16) for m in (first, second, gather, leave, place)]


def pack_kernel(tok, cot, sel, idx, strip, kept, packed, tok_in, cot_in, sel_in, idx_in, rows, sems):
    copies = [
        pltpu.make_async_copy(src, dst, sems.at[k])
        for k, (src, dst) in enumerate(
            ((tok, tok_in), (cot, cot_in), (sel, sel_in), (idx, idx_in))
        )
    ]
    for copy in copies:
        copy.start()
    for arr, ref in enumerate((tok_in, cot_in)):
        copies[arr].wait()
        for k in range(72):
            at = arr * T + 2 * k
            rows[at : at + 2, :] = ref[k // 12, k % 12].astype(F32)
    copies[2].wait()
    out = dot(sel_in[...], rows[...].astype(BF16)).astype(BF16)
    strip[...] = out[0:T]
    kept[...] = out[T:]
    copies[3].wait()
    packed[0:T, :] = idx_in[:, 0:128]
    packed[T:PACK, :] = packed_rows(idx_in)


def repack_kernel(kept, arrived, sel, strip):
    strip[...] = (dot(sel[0], kept[...]) + dot(sel[1], arrived[...])).astype(BF16)


def unpack_kernel(kept, first, second, sel, out, rows):
    total = dot(sel[0], kept[0]) + dot(sel[1], first[0])
    rows[...] = total + dot(sel[2], second[0]) + dot(sel[3], second[1])
    for k in range(72):
        out[k // 12, k % 12] = rows[2 * k : 2 * k + 2, :].astype(BF16)


def mix_kernel(parts, scattered, out, wide):
    n, rows, _ = out.shape
    bias_rows = scattered.shape[0] // n
    rows = rows - bias_rows
    wide[...] = jnp.sum(parts[...].astype(F32), axis=0)
    for k in range(n):
        mine = wide[rows * k : rows * k + rows, :]
        theirs = scattered[bias_rows * k : bias_rows * k + bias_rows, :]
        out[k] = jnp.concatenate((mine, theirs), axis=0).astype(BF16)


def sum_kernel(parts, out):
    total = jnp.sum(parts[...].astype(F32), axis=0).astype(BF16)
    for k in range(out.shape[0]):
        out[k] = total


def split_kernel(parts, out, scattered, wide):
    n = parts.shape[0]
    bias_rows = scattered.shape[0] // n
    rows = parts.shape[1] - bias_rows
    for k in range(n):
        part = parts[k].astype(F32)
        wide[rows * k : rows * k + rows, :] = part[0:rows]
        scattered[bias_rows * k : bias_rows * k + bias_rows, :] = part[rows:]
    total = wide[...].astype(BF16)
    for k in range(out.shape[0]):
        out[k] = total


def finish_kernel(parts, qkv, proj):
    wide = parts[...].reshape(6 * C, 128).astype(F32)
    for k in range(4):
        qkv[:, 128 * k : 128 * k + 128] = wide[C * k : C * k + C]
    qkv[:, 512:576] = wide[4 * C : 5 * C, 0:64]
    proj[:, 0:64] = wide[4 * C : 5 * C, 64:128]
    proj[:, 64:C] = wide[5 * C : 6 * C]


def packed_rows(idx):
    lane = lax.broadcasted_iota(jnp.int32, (24, 128), 1)
    tail = jnp.zeros((24, 128), jnp.int32)
    for c in range(6):
        part = jnp.concatenate(
            (idx[24 * c : 24 * c + 24, 128:T], jnp.zeros((24, 112), jnp.int32)), axis=1
        )
        part = pltpu.roll(part, 16 * c, 1) if c else part
        tail = jnp.where((lane >= 16 * c) & (lane < 16 * c + 16), part, tail)
    return tail


def bias_body(first, table, col, row, packed, bias, flat):
    def block(i, carry):
        at = pl.ds(pl.multiple_of(i * 8, 8), 8)
        position = packed[at, :]
        low = position & 127
        high = position >> 7
        totals = [jnp.zeros((8, 128), F32)] * HALF
        for k in range(BLKS):
            here = high == k
            for h in range(HALF):
                r = (first + h) * BLKS + k
                values = jnp.broadcast_to(table[r : r + 1, :], (8, 128))
                found = jnp.take_along_axis(values, low, axis=1, mode="promise_in_bounds")
                totals[h] = jnp.where(here, found, totals[h])
        for h in range(HALF):
            flat[h, at, :] = totals[h]
        return carry

    lax.fori_loop(0, PACK // 8, block, 0, unroll=7)
    same = col[...] == row[...]
    for h in range(HALF):
        bias[h, :, 0:128] = jnp.where(same[:, 0:128], flat[h, 0:T, :], -1e9)
        tail = flat[h, T:PACK, :]
        for c in range(6):
            part = pltpu.roll(tail, 128 - 16 * c, 1) if c else tail
            at = slice(24 * c, 24 * c + 24)
            bias[h, at, 128:T] = jnp.where(same[at, 128:T], part[:, 0:16], -1e9)


def bias_first_kernel(packed, table, col, row, bias, flat):
    bias_body(0, table, col, row, packed, bias, flat)


def bias_second_kernel(packed, table, col, row, bias, flat):
    bias_body(HALF, table, col, row, packed, bias, flat)


def main_kernel(kept, lon, lat, sel, bias_a, bias_b, wqkv, wproj,
                grads, ds_out, grad_in_out, normed_out, inv_std_out, cot_out, ds_tail):
    scale = HD ** (-0.5)
    both = dot(sel[0], kept[...]) + dot(sel[1], lon[...]) + dot(sel[2], lat[...])
    values = both[0:T]
    cot = both[T:].astype(BF16)
    center = values - jnp.mean(values, axis=-1, keepdims=True)
    inv_std = lax.rsqrt(jnp.mean(center * center, axis=-1, keepdims=True) + 1e-05)
    normed = center * inv_std
    hidden = normed.astype(BF16)
    proj = dot(hidden, wqkv[...])
    query = proj[:, 0:C]
    query_t = query.T.astype(BF16)
    query = query.astype(BF16)
    key = proj[:, C : 2 * C].astype(BF16)
    value = proj[:, 2 * C :].astype(BF16)
    att = dot(cot, wproj[...], 1, 1)
    att_t = att.T.astype(BF16)
    att = att.astype(BF16)
    head = lax.broadcasted_iota(jnp.int32, (T, C), 1) // HD
    zero = jnp.zeros((T, C), BF16)
    attended = jnp.zeros((T, C), F32)
    grad_query = jnp.zeros((T, C), F32)
    key_t = []
    value_t = []
    lane = lax.broadcasted_iota(jnp.int32, (24, 128), 1)
    masks = [head == h for h in range(HEADS)]
    scores = [dot(jnp.where(m, query, zero), key, 1, 1) * scale for m in masks]
    grad_probs = [dot(jnp.where(m, att, zero), value, 1, 1) for m in masks]
    probs = []
    for h in range(HEADS):
        score = scores[h] + (bias_a[h] if h < HALF else bias_b[h - HALF])
        exponent = jnp.exp(score - jnp.max(score, axis=-1, keepdims=True))
        probs.append(exponent * (1.0 / jnp.sum(exponent, axis=-1, keepdims=True)))
    for h in range(HEADS):
        prob_half = probs[h].astype(BF16)
        attended = attended + dot(prob_half, jnp.where(masks[h], value, zero))
        value_t.append(dot(att_t[HD * h : HD * h + HD], prob_half))
    for h in range(HEADS):
        prob, grad_prob = probs[h], grad_probs[h]
        ds = prob * (grad_prob - jnp.sum(grad_prob * prob, axis=-1, keepdims=True))
        ds_half = ds.astype(BF16)
        grad_query = grad_query + dot(ds_half, jnp.where(masks[h], key, zero))
        key_t.append(dot(query_t[HD * h : HD * h + HD], ds_half))
        ds_out[h, 0:T, :] = ds[:, 0:128]
        ds_tail[:, 0:16] = ds[:, 128:T]
        packed = jnp.zeros((24, 128), F32)
        for c in range(6):
            part = ds_tail[24 * c : 24 * c + 24, :]
            part = pltpu.roll(part, 16 * c, 1) if c else part
            packed = jnp.where((lane >= 16 * c) & (lane < 16 * c + 16), part, packed)
        ds_out[h, T:PACK, :] = packed
    grad_key = jnp.concatenate(key_t, axis=0).T
    grad_value = jnp.concatenate(value_t, axis=0).T
    grad_in = jnp.concatenate((grad_query * scale, grad_key * scale, grad_value), axis=1)
    grad_in = grad_in.astype(BF16)
    grad_qkv = dot(hidden, grad_in, 0, 0)
    grad_proj = dot(attended.astype(BF16), cot, 0, 0)
    both = jnp.concatenate((grad_qkv, grad_proj), axis=1).astype(BF16)
    for k in range(6):
        grads[C * k : C * k + C, :] = both[:, 128 * k : 128 * k + 128]
    grad_in_out[...] = grad_in
    normed_out[...] = normed
    inv_std_out[...] = inv_std
    cot_out[...] = cot


def norm_kernel(grad_in, normed_ref, inv_std, cot, wqkv, leave, ret_kept, ret_strip):
    normed = normed_ref[...]
    grad_hidden = dot(grad_in[...], wqkv[...], 1, 1)
    grad_norm = inv_std[...] * (
        grad_hidden
        - jnp.mean(grad_hidden, axis=-1, keepdims=True)
        - normed * jnp.mean(grad_hidden * normed, axis=-1, keepdims=True)
    )
    returned = (cot[...].astype(F32) + grad_norm).astype(BF16)
    parts = dot(leave[...], returned).astype(BF16)
    for k in range(2):
        ret_kept[k] = parts[40 * k : 40 * k + 40]
        ret_strip[k] = parts[80 + 40 * k : 120 + 40 * k]


def scatter_kernel(packed, ds, out, total):
    total[...] = jnp.zeros_like(total)
    blocks = lax.broadcasted_iota(jnp.int32, (32, 128), 0).astype(F32).astype(BF16)
    lows = lax.broadcasted_iota(jnp.int32, (128, 128), 0).astype(F32).astype(BF16)
    one = jnp.ones((128, 128), BF16)
    none = jnp.zeros((128, 128), BF16)

    def block(i, carry):
        at = pl.ds(pl.multiple_of(i * 8, 8), 8)
        position = packed[at, :]
        low = (position & 127).astype(F32)
        high = (position >> 7).astype(F32)
        left = []
        right = []
        for r in range(8):
            low_row = jnp.broadcast_to(low[r : r + 1], (16, 128)).astype(BF16)
            high_row = jnp.broadcast_to(high[r : r + 1], (16, 128)).astype(BF16)
            right.append(
                jnp.concatenate(
                    [
                        jnp.where(lows[16 * k : 16 * k + 16] == low_row, one[0:16], none[0:16])
                        for k in range(8)
                    ],
                    axis=0,
                )
            )
            mine = [blocks[16 * k : 16 * k + 16] == high_row for k in range(2)]
            parts = []
            for h in range(HEADS):
                row = jnp.broadcast_to(ds[h, at, :][r : r + 1], (16, 128)).astype(BF16)
                parts += [jnp.where(m, row, none[0:16]) for m in mine]
            left.append(jnp.concatenate(parts, axis=0))
        total[...] += dot(jnp.concatenate(left, axis=1), jnp.concatenate(right, axis=1), 1, 1)
        return carry

    lax.fori_loop(0, PACK // 8, block, 0, unroll=7)
    out[...] = total[...]


def call(kernel, shapes, scratch, cost, *args, copies=0):
    scratch = [pltpu.VMEM(s, d) for s, d in scratch]
    specs = {}
    if copies:
        scratch.append(pltpu.SemaphoreType.DMA((copies,)))
        specs["in_specs"] = [pl.BlockSpec(memory_space=pltpu.MemorySpace.HBM)] * copies
    if copies:
        args = [pltpu.with_memory_space_constraint(a, pltpu.MemorySpace.HBM) for a in args]
    return pl.pallas_call(
        kernel,
        out_shape=[jax.ShapeDtypeStruct(s, d) for s, d in shapes],
        scratch_shapes=scratch,
        compiler_params=pltpu.CompilerParams(vmem_limit_bytes=(48 if copies else 48) << 20),
        cost_estimate=pl.CostEstimate(flops=cost, bytes_accessed=1 << 20, transcendentals=0),
        **specs,
    )(*args)


def exchange(block, axes, groups=None):
    return lax.all_to_all(block, axes, 0, 0, axis_index_groups=groups, tiled=False)


def local(sizes, tokens, cotangent, region, pos_index, w_qkv, w_proj, bias_table):
    n_lon, n_lat, n_y = sizes
    n_z = n_lon // n_y
    first, second, gather, leave, place = selections()
    across = ("lat", "rep")

    def moved(block, axes, n, distance):
        return lax.ppermute(block, axes, [((i + distance) % n, i) for i in range(n)])

    table = jnp.pad(bias_table.reshape(ROWS, HEADS).T, ((0, 0), (0, BLKS * 128 - ROWS)))
    table = table.reshape(HEADS * BLKS, 128)

    col, row = region.reshape(T, 1), region.reshape(1, T)
    bias_shape = ((HALF, T, T), F32)
    bias_scratch = [((HALF, PACK, 128), F32)]
    block = ((T, C), BF16)
    order = (1, 2, 0, 3)
    stored = ((6, 12, 2, C), BF16)
    strip, kept, packed = call(
        pack_kernel,
        [block] * 2 + [((PACK, 128), jnp.int32)],
        [stored, stored, ((2 * T, 2 * T), BF16), ((T, T), jnp.int32), ((2 * T, C), F32)],
        10**8,
        tokens.transpose(order), cotangent.transpose(order), first, pos_index,
        copies=4,
    )
    lon = moved(strip, "lon", n_lon, 1)
    (bias_a,) = call(
        bias_first_kernel, [bias_shape], bias_scratch, 3 * 10**9, packed, table, col, row
    )
    (strip,) = call(repack_kernel, [block], [], 10**8, kept, lon, second)
    strip, late_packed = lax.optimization_barrier((strip, packed))
    lat = moved(strip, across, n_lat, 1)
    (bias_b,) = call(
        bias_second_kernel, [bias_shape], bias_scratch, 3 * 10**9, late_packed, table, col, row
    )
    grads, ds, grad_in, normed, inv_std, cot = call(
        main_kernel,
        [
            ((6 * C, 128), BF16),
            ((HEADS, PACK, 128), F32),
            ((T, 3 * C), BF16),
            ((T, C), F32),
            ((T, 1), F32),
            block,
        ],
        [((T, 128), F32)],
        10**10,
        kept, lon, lat, gather, bias_a, bias_b, w_qkv, w_proj,
    )
    rows_y = [[z * n_y + y for y in range(n_y)] for z in range(n_z)]
    rows_z = [[z * n_y + y for z in range(n_z)] for y in range(n_y)]
    rows = 6 * C // n_lat
    grads = exchange(grads.reshape(n_lat, rows, 128), across)
    (scattered,) = call(
        scatter_kernel, [((192, 128), F32)], [((192, 128), F32)], 5 * 10**9, packed, ds
    )
    mixed_rows = (rows + 192) // n_y
    wide = [((rows, 128), F32)]
    (mixed,) = call(
        mix_kernel, [((n_y, mixed_rows, 128), BF16)], wide, 10**7, grads, scattered
    )
    mixed, grad_in = lax.optimization_barrier((mixed, grad_in))
    quarter = ((2, 40, C), BF16)
    ret_kept, ret_strip = call(
        norm_kernel, [quarter] * 2, [], 10**8, grad_in, normed, inv_std, cot, w_qkv, leave
    )
    ret_first = moved(ret_strip, across, n_lat, -1)
    mixed = exchange(mixed, "lon", rows_y)
    (mixed,) = call(sum_kernel, [((n_z, mixed_rows, 128), BF16)], [], 10**7, mixed)
    mixed = exchange(mixed, "lon", rows_z)
    (mixed,) = call(sum_kernel, [((n_y, mixed_rows, 128), BF16)], [], 10**7, mixed)
    mixed, ret_first = lax.optimization_barrier((mixed, ret_first))
    ret_second = moved(jnp.stack((ret_kept[1], ret_first[1])), "lon", n_lon, -1)
    mixed = exchange(mixed, "lon", rows_y)
    grads, scattered = call(
        split_kernel, [((n_lat, rows, 128), BF16), ((192, 128), F32)], wide, 10**7, mixed
    )
    grads, ret_second = lax.optimization_barrier((grads, ret_second))
    grads = exchange(grads, across)
    (grad_tokens,) = call(
        unpack_kernel, [((6, 12, 2, C), BF16)], [((T, C), F32)], 10**8,
        ret_kept, ret_first, ret_second, place,
    )
    scattered = scattered.reshape(HEADS, 32 * 128)
    grad_bias = scattered[:, :ROWS].T.reshape(ROWS, 1, HEADS)
    grad_qkv, grad_proj = call(
        finish_kernel, [((C, 3 * C), F32), ((C, C), F32)], [], 10**7, grads
    )
    return (grad_tokens.transpose(2, 0, 1, 3), grad_qkv, grad_proj, grad_bias)


def solution(mesh):
    n_lon = mesh.shape["lon"]
    n_lat = mesh.shape["lat"] * mesh.shape["rep"]
    n_y = 8 if n_lon % 8 == 0 else 2
    placed = (
        P(None, ("lat", "rep"), "lon", None),
        P(None, ("lat", "rep"), "lon", None),
        P(None, ("lat", "rep"), "lon"),
        P(),
        P(),
        P(),
        P(None, ("lat", "rep"), None),
    )
    return jax.shard_map(
        functools.partial(local, (n_lon, n_lat, n_y)),
        mesh=mesh,
        in_specs=placed,
        out_specs=(P(None, ("lat", "rep"), "lon", None), P(), P(), P(None, ("lat", "rep"), None)),
        check_vma=False,
    )
```

```python
import functools

import jax
import jax.numpy as jnp
import numpy as np
from jax import lax
from jax.experimental import pallas as pl
from jax.experimental.pallas import tpu as pltpu
from jax.sharding import PartitionSpec as P

F32 = jnp.float32
BF16 = jnp.bfloat16
T = 144
C = 192
HEADS = 6
HD = 32
ROWS = 3312
BLKS = 26
PACK = 168
HALF = HEADS // 2


def dot(a, b, ca=1, cb=0):
    return lax.dot_general(a, b, (((ca,), (cb,)), ((), ())), preferred_element_type=F32)


def selections():
    first = np.zeros((288, 288), np.float32)
    second = np.zeros((2, 144, 144), np.float32)
    gather = np.zeros((3, 288, 144), np.float32)
    leave = np.zeros((160, 144), np.float32)
    place = np.zeros((4, T, 40), np.float32)
    for p in range(2):
        for a in range(6):
            for b in range(12):
                slab = (a * 12 + b) * 2 + (p + 1) % 2
                half = (p * 6 + a) * 6 + b % 6
                wide = (p * 3 + a % 3) * 12 + (b + 6) % 12
                for arr in range(2):
                    first[(0 if b < 6 else 144) + arr * 72 + half, arr * T + slab] = 1
                    source = 1 if b < 6 else 0
                    if a < 3:
                        second[source, arr * 72 + wide, arr * 72 + half] = 1
                    else:
                        token = (p * 6 + a - 3) * 12 + (b + 6) % 12
                        gather[source, arr * 144 + token, arr * 72 + half] = 1
                token = (p * 6 + a) * 12 + b
                if a >= 3:
                    for arr in range(2):
                        row = (p * 3 + a - 3) * 12 + b
                        gather[2, arr * 144 + token, arr * 72 + row] = 1
                row = (p * 3 + a % 3) * 6 + b % 6
                leave[(80 if a >= 3 else 0) + (40 if b >= 6 else 0) + row, token] = 1
                home = (((a + 3) % 6) * 12 + (b + 6) % 12) * 2 + (p + 1) % 2
                place[(2 if b >= 6 else 0) + (1 if a >= 3 else 0), home, row] = 1
    return [jnp.asarray(m, BF16) for m in (first, second, gather, leave, place)]


def pack_kernel(tok, cot, sel, idx, strip, kept, packed, tok_in, cot_in, sel_in, idx_in, rows, sems):
    copies = [
        pltpu.make_async_copy(src, dst, sems.at[k])
        for k, (src, dst) in enumerate(
            ((tok, tok_in), (cot, cot_in), (sel, sel_in), (idx, idx_in))
        )
    ]
    for copy in copies:
        copy.start()
    for arr, ref in enumerate((tok_in, cot_in)):
        copies[arr].wait()
        for k in range(72):
            at = arr * T + 2 * k
            rows[at : at + 2, :] = ref[k // 12, k % 12].astype(F32)
    copies[2].wait()
    out = dot(sel_in[...], rows[...].astype(BF16)).astype(BF16)
    strip[...] = out[0:T]
    kept[...] = out[T:]
    copies[3].wait()
    packed[0:T, :] = idx_in[:, 0:128]
    packed[T:PACK, :] = packed_rows(idx_in)


def repack_kernel(kept, arrived, sel, strip):
    strip[...] = (dot(sel[0], kept[...]) + dot(sel[1], arrived[...])).astype(BF16)


def unpack_kernel(kept, first, second, sel, out, rows):
    total = dot(sel[0], kept[0]) + dot(sel[1], first[0])
    rows[...] = total + dot(sel[2], second[0]) + dot(sel[3], second[1])
    for k in range(72):
        out[k // 12, k % 12] = rows[2 * k : 2 * k + 2, :].astype(BF16)


def mix_kernel(parts, scattered, out, wide):
    n, rows, _ = out.shape
    bias_rows = scattered.shape[0] // n
    rows = rows - bias_rows
    wide[...] = jnp.sum(parts[...].astype(F32), axis=0)
    for k in range(n):
        mine = wide[rows * k : rows * k + rows, :]
        theirs = scattered[bias_rows * k : bias_rows * k + bias_rows, :]
        out[k] = jnp.concatenate((mine, theirs), axis=0).astype(BF16)


def sum_kernel(parts, out):
    total = jnp.sum(parts[...].astype(F32), axis=0).astype(BF16)
    for k in range(out.shape[0]):
        out[k] = total


def split_kernel(parts, out, scattered, wide):
    n = parts.shape[0]
    bias_rows = scattered.shape[0] // n
    rows = parts.shape[1] - bias_rows
    for k in range(n):
        part = parts[k].astype(F32)
        wide[rows * k : rows * k + rows, :] = part[0:rows]
        scattered[bias_rows * k : bias_rows * k + bias_rows, :] = part[rows:]
    total = wide[...].astype(BF16)
    for k in range(out.shape[0]):
        out[k] = total


def finish_kernel(parts, qkv, proj):
    wide = parts[...].reshape(6 * C, 128).astype(F32)
    for k in range(4):
        qkv[:, 128 * k : 128 * k + 128] = wide[C * k : C * k + C]
    qkv[:, 512:576] = wide[4 * C : 5 * C, 0:64]
    proj[:, 0:64] = wide[4 * C : 5 * C, 64:128]
    proj[:, 64:C] = wide[5 * C : 6 * C]


def packed_rows(idx):
    lane = lax.broadcasted_iota(jnp.int32, (24, 128), 1)
    tail = jnp.zeros((24, 128), jnp.int32)
    for c in range(6):
        part = jnp.concatenate(
            (idx[24 * c : 24 * c + 24, 128:T], jnp.zeros((24, 112), jnp.int32)), axis=1
        )
        part = pltpu.roll(part, 16 * c, 1) if c else part
        tail = jnp.where((lane >= 16 * c) & (lane < 16 * c + 16), part, tail)
    return tail


def bias_body(first, table, col, row, packed, bias, flat):
    def block(i, carry):
        at = pl.ds(pl.multiple_of(i * 8, 8), 8)
        position = packed[at, :]
        low = position & 127
        high = position >> 7
        totals = [jnp.zeros((8, 128), F32)] * HALF
        for k in range(BLKS):
            here = high == k
            for h in range(HALF):
                r = (first + h) * BLKS + k
                values = jnp.broadcast_to(table[r : r + 1, :], (8, 128))
                found = jnp.take_along_axis(values, low, axis=1, mode="promise_in_bounds")
                totals[h] = jnp.where(here, found, totals[h])
        for h in range(HALF):
            flat[h, at, :] = totals[h]
        return carry

    lax.fori_loop(0, PACK // 8, block, 0, unroll=7)
    same = col[...] == row[...]
    for h in range(HALF):
        bias[h, :, 0:128] = jnp.where(same[:, 0:128], flat[h, 0:T, :], -1e9)
        tail = flat[h, T:PACK, :]
        for c in range(6):
            part = pltpu.roll(tail, 128 - 16 * c, 1) if c else tail
            at = slice(24 * c, 24 * c + 24)
            bias[h, at, 128:T] = jnp.where(same[at, 128:T], part[:, 0:16], -1e9)


def bias_first_kernel(packed, table, col, row, bias, flat):
    bias_body(0, table, col, row, packed, bias, flat)


def bias_second_kernel(packed, table, col, row, bias, flat):
    bias_body(HALF, table, col, row, packed, bias, flat)


def main_kernel(kept, lon, lat, sel, bias_a, bias_b, wqkv, wproj,
                grads, ds_out, grad_in_out, normed_out, inv_std_out, cot_out):
    scale = HD ** (-0.5)
    both = dot(sel[0], kept[...]) + dot(sel[1], lon[...]) + dot(sel[2], lat[...])
    values = both[0:T]
    cot = both[T:].astype(BF16)
    center = values - jnp.mean(values, axis=-1, keepdims=True)
    inv_std = lax.rsqrt(jnp.mean(center * center, axis=-1, keepdims=True) + 1e-05)
    normed = center * inv_std
    hidden = normed.astype(BF16)
    proj = dot(hidden, wqkv[...])
    query = proj[:, 0:C]
    query_t = query.T.astype(BF16)
    query = query.astype(BF16)
    key = proj[:, C : 2 * C].astype(BF16)
    value = proj[:, 2 * C :].astype(BF16)
    att = dot(cot, wproj[...], 1, 1)
    att_t = att.T.astype(BF16)
    att = att.astype(BF16)
    head = lax.broadcasted_iota(jnp.int32, (T, C), 1) // HD
    zero = jnp.zeros((T, C), BF16)
    attended = jnp.zeros((T, C), F32)
    grad_query = jnp.zeros((T, C), F32)
    key_t = []
    value_t = []
    masks = [head == h for h in range(HEADS)]
    scores = [dot(jnp.where(m, query, zero), key, 1, 1) * scale for m in masks]
    grad_probs = [dot(jnp.where(m, att, zero), value, 1, 1) for m in masks]
    probs = []
    for h in range(HEADS):
        score = scores[h] + (bias_a[h] if h < HALF else bias_b[h - HALF])
        exponent = jnp.exp(score - jnp.max(score, axis=-1, keepdims=True))
        probs.append(exponent * (1.0 / jnp.sum(exponent, axis=-1, keepdims=True)))
    for h in range(HEADS):
        prob_half = probs[h].astype(BF16)
        attended = attended + dot(prob_half, jnp.where(masks[h], value, zero))
        value_t.append(dot(att_t[HD * h : HD * h + HD], prob_half))
    for h in range(HEADS):
        prob, grad_prob = probs[h], grad_probs[h]
        ds = prob * (grad_prob - jnp.sum(grad_prob * prob, axis=-1, keepdims=True))
        ds_half = ds.astype(BF16)
        grad_query = grad_query + dot(ds_half, jnp.where(masks[h], key, zero))
        key_t.append(dot(query_t[HD * h : HD * h + HD], ds_half))
        ds_out[h] = ds
    grad_key = jnp.concatenate(key_t, axis=0).T
    grad_value = jnp.concatenate(value_t, axis=0).T
    grad_in = jnp.concatenate((grad_query * scale, grad_key * scale, grad_value), axis=1)
    grad_in = grad_in.astype(BF16)
    grad_qkv = dot(hidden, grad_in, 0, 0)
    grad_proj = dot(attended.astype(BF16), cot, 0, 0)
    both = jnp.concatenate((grad_qkv, grad_proj), axis=1).astype(BF16)
    for k in range(6):
        grads[C * k : C * k + C, :] = both[:, 128 * k : 128 * k + 128]
    grad_in_out[...] = grad_in
    normed_out[...] = normed
    inv_std_out[...] = inv_std
    cot_out[...] = cot


def norm_kernel(grad_in, normed_ref, inv_std, cot, wqkv, leave, ret_kept, ret_strip):
    normed = normed_ref[...]
    grad_hidden = dot(grad_in[...], wqkv[...], 1, 1)
    grad_norm = inv_std[...] * (
        grad_hidden
        - jnp.mean(grad_hidden, axis=-1, keepdims=True)
        - normed * jnp.mean(grad_hidden * normed, axis=-1, keepdims=True)
    )
    returned = (cot[...].astype(F32) + grad_norm).astype(BF16)
    parts = dot(leave[...], returned).astype(BF16)
    for k in range(2):
        ret_kept[k] = parts[40 * k : 40 * k + 40]
        ret_strip[k] = parts[80 + 40 * k : 120 + 40 * k]


def scatter_kernel(packed, ds_in, out, total, ds, raw):
    lane = lax.broadcasted_iota(jnp.int32, (24, 128), 1)
    for h in range(HEADS):
        ds[h, 0:T, :] = ds_in[h, :, 0:128]
        raw[h, :, 0:16] = ds_in[h, :, 128:T]
    for h in range(HEADS):
        tail = jnp.zeros((24, 128), F32)
        for c in range(6):
            part = raw[h, 24 * c : 24 * c + 24, :]
            part = pltpu.roll(part, 16 * c, 1) if c else part
            tail = jnp.where((lane >= 16 * c) & (lane < 16 * c + 16), part, tail)
        ds[h, T:PACK, :] = tail
    total[...] = jnp.zeros_like(total)
    blocks = lax.broadcasted_iota(jnp.int32, (32, 128), 0).astype(F32).astype(BF16)
    lows = lax.broadcasted_iota(jnp.int32, (128, 128), 0).astype(F32).astype(BF16)
    one = jnp.ones((128, 128), BF16)
    none = jnp.zeros((128, 128), BF16)

    def block(i, carry):
        at = pl.ds(pl.multiple_of(i * 8, 8), 8)
        position = packed[at, :]
        low = (position & 127).astype(F32)
        high = (position >> 7).astype(F32)
        left = []
        right = []
        for r in range(8):
            low_row = jnp.broadcast_to(low[r : r + 1], (16, 128)).astype(BF16)
            high_row = jnp.broadcast_to(high[r : r + 1], (16, 128)).astype(BF16)
            right.append(
                jnp.concatenate(
                    [
                        jnp.where(lows[16 * k : 16 * k + 16] == low_row, one[0:16], none[0:16])
                        for k in range(8)
                    ],
                    axis=0,
                )
            )
            mine = [blocks[16 * k : 16 * k + 16] == high_row for k in range(2)]
            parts = []
            for h in range(HEADS):
                row = jnp.broadcast_to(ds[h, at, :][r : r + 1], (16, 128)).astype(BF16)
                parts += [jnp.where(m, row, none[0:16]) for m in mine]
            left.append(jnp.concatenate(parts, axis=0))
        total[...] += dot(jnp.concatenate(left, axis=1), jnp.concatenate(right, axis=1), 1, 1)
        return carry

    lax.fori_loop(0, PACK // 8, block, 0, unroll=7)
    out[...] = total[...]


def call(kernel, shapes, scratch, cost, *args, copies=0):
    scratch = [pltpu.VMEM(s, d) for s, d in scratch]
    specs = {}
    if copies:
        scratch.append(pltpu.SemaphoreType.DMA((copies,)))
        specs["in_specs"] = [pl.BlockSpec(memory_space=pltpu.MemorySpace.HBM)] * copies
    if copies:
        args = [pltpu.with_memory_space_constraint(a, pltpu.MemorySpace.HBM) for a in args]
    return pl.pallas_call(
        kernel,
        out_shape=[jax.ShapeDtypeStruct(s, d) for s, d in shapes],
        scratch_shapes=scratch,
        compiler_params=pltpu.CompilerParams(vmem_limit_bytes=(48 if copies else 48) << 20),
        cost_estimate=pl.CostEstimate(flops=cost, bytes_accessed=1 << 20, transcendentals=0),
        **specs,
    )(*args)


def exchange(block, axes, groups=None):
    return lax.all_to_all(block, axes, 0, 0, axis_index_groups=groups, tiled=False)


def local(sizes, tokens, cotangent, region, pos_index, w_qkv, w_proj, bias_table):
    n_lon, n_lat, n_y = sizes
    n_z = n_lon // n_y
    first, second, gather, leave, place = selections()
    across = ("lat", "rep")

    def moved(block, axes, n, distance):
        return lax.ppermute(block, axes, [((i + distance) % n, i) for i in range(n)])

    table = jnp.pad(bias_table.reshape(ROWS, HEADS).T, ((0, 0), (0, BLKS * 128 - ROWS)))
    table = table.reshape(HEADS * BLKS, 128)

    col, row = region.reshape(T, 1), region.reshape(1, T)
    bias_shape = ((HALF, T, T), F32)
    bias_scratch = [((HALF, PACK, 128), F32)]
    block = ((T, C), BF16)
    order = (1, 2, 0, 3)
    stored = ((6, 12, 2, C), BF16)
    strip, kept, packed = call(
        pack_kernel,
        [block] * 2 + [((PACK, 128), jnp.int32)],
        [stored, stored, ((2 * T, 2 * T), BF16), ((T, T), jnp.int32), ((2 * T, C), F32)],
        10**8,
        tokens.transpose(order), cotangent.transpose(order), first, pos_index,
        copies=4,
    )
    lon = moved(strip, "lon", n_lon, 1)
    (bias_a,) = call(
        bias_first_kernel, [bias_shape], bias_scratch, 3 * 10**9, packed, table, col, row
    )
    (strip,) = call(repack_kernel, [block], [], 10**8, kept, lon, second)
    strip, late_packed = lax.optimization_barrier((strip, packed))
    lat = moved(strip, across, n_lat, 1)
    (bias_b,) = call(
        bias_second_kernel, [bias_shape], bias_scratch, 3 * 10**9, late_packed, table, col, row
    )
    grads, ds, grad_in, normed, inv_std, cot = call(
        main_kernel,
        [
            ((6 * C, 128), BF16),
            ((HEADS, T, T), F32),
            ((T, 3 * C), BF16),
            ((T, C), F32),
            ((T, 1), F32),
            block,
        ],
        [],
        10**10,
        kept, lon, lat, gather, bias_a, bias_b, w_qkv, w_proj,
    )
    rows_y = [[z * n_y + y for y in range(n_y)] for z in range(n_z)]
    rows_z = [[z * n_y + y for z in range(n_z)] for y in range(n_y)]
    rows = 6 * C // n_lat
    grads = exchange(grads.reshape(n_lat, rows, 128), across)
    (scattered,) = call(
        scatter_kernel, [((192, 128), F32)],
        [((192, 128), F32), ((HEADS, PACK, 128), F32), ((HEADS, T, 128), F32)],
        5 * 10**9,
        packed, ds,
    )
    quarter = ((2, 40, C), BF16)
    ret_kept, ret_strip = call(
        norm_kernel, [quarter] * 2, [], 10**8, grad_in, normed, inv_std, cot, w_qkv, leave
    )
    scattered, ret_strip = lax.optimization_barrier((scattered, ret_strip))
    ret_first = moved(ret_strip, across, n_lat, -1)
    mixed_rows = (rows + 192) // n_y
    wide = [((rows, 128), F32)]
    (mixed,) = call(
        mix_kernel, [((n_y, mixed_rows, 128), BF16)], wide, 10**7, grads, scattered
    )
    mixed, ret_first = lax.optimization_barrier((mixed, ret_first))
    mixed = exchange(mixed, "lon", rows_y)
    (mixed,) = call(sum_kernel, [((n_z, mixed_rows, 128), BF16)], [], 10**7, mixed)
    mixed = exchange(mixed, "lon", rows_z)
    (mixed,) = call(sum_kernel, [((n_y, mixed_rows, 128), BF16)], [], 10**7, mixed)
    mixed, ret_kept = lax.optimization_barrier((mixed, ret_kept))
    ret_second = moved(jnp.stack((ret_kept[1], ret_first[1])), "lon", n_lon, -1)
    mixed = exchange(mixed, "lon", rows_y)
    grads, scattered = call(
        split_kernel, [((n_lat, rows, 128), BF16), ((192, 128), F32)], wide, 10**7, mixed
    )
    grads, ret_second = lax.optimization_barrier((grads, ret_second))
    grads = exchange(grads, across)
    (grad_tokens,) = call(
        unpack_kernel, [((6, 12, 2, C), BF16)], [((T, C), F32)], 10**8,
        ret_kept, ret_first, ret_second, place,
    )
    scattered = scattered.reshape(HEADS, 32 * 128)
    grad_bias = scattered[:, :ROWS].T.reshape(ROWS, 1, HEADS)
    grad_qkv, grad_proj = call(
        finish_kernel, [((C, 3 * C), F32), ((C, C), F32)], [], 10**7, grads
    )
    return (grad_tokens.transpose(2, 0, 1, 3), grad_qkv, grad_proj, grad_bias)


def solution(mesh):
    n_lon = mesh.shape["lon"]
    n_lat = mesh.shape["lat"] * mesh.shape["rep"]
    n_y = 8 if n_lon % 8 == 0 else 2
    placed = (
        P(None, ("lat", "rep"), "lon", None),
        P(None, ("lat", "rep"), "lon", None),
        P(None, ("lat", "rep"), "lon"),
        P(),
        P(),
        P(),
        P(None, ("lat", "rep"), None),
    )
    return jax.shard_map(
        functools.partial(local, (n_lon, n_lat, n_y)),
        mesh=mesh,
        in_specs=placed,
        out_specs=(P(None, ("lat", "rep"), "lon", None), P(), P(), P(None, ("lat", "rep"), None)),
        check_vma=False,
    )
```

```python
import functools

import jax
import jax.numpy as jnp
import numpy as np
from jax import lax
from jax.experimental import pallas as pl
from jax.experimental.pallas import tpu as pltpu
from jax.sharding import PartitionSpec as P

F32 = jnp.float32
BF16 = jnp.bfloat16
T = 144
C = 192
HEADS = 6
HD = 32
ROWS = 3312
BLKS = 26
PACK = 168
HALF = HEADS // 2


def dot(a, b, ca=1, cb=0):
    return lax.dot_general(a, b, (((ca,), (cb,)), ((), ())), preferred_element_type=F32)


def selections():
    first = np.zeros((288, 288), np.float32)
    second = np.zeros((2, 144, 144), np.float32)
    gather = np.zeros((3, 288, 144), np.float32)
    leave = np.zeros((160, 144), np.float32)
    place = np.zeros((4, T, 40), np.float32)
    for p in range(2):
        for a in range(6):
            for b in range(12):
                slab = (a * 12 + b) * 2 + (p + 1) % 2
                half = (p * 6 + a) * 6 + b % 6
                wide = (p * 3 + a % 3) * 12 + (b + 6) % 12
                for arr in range(2):
                    first[(0 if b < 6 else 144) + arr * 72 + half, arr * T + slab] = 1
                    source = 1 if b < 6 else 0
                    if a < 3:
                        second[source, arr * 72 + wide, arr * 72 + half] = 1
                    else:
                        token = (p * 6 + a - 3) * 12 + (b + 6) % 12
                        gather[source, arr * 144 + token, arr * 72 + half] = 1
                token = (p * 6 + a) * 12 + b
                if a >= 3:
                    for arr in range(2):
                        row = (p * 3 + a - 3) * 12 + b
                        gather[2, arr * 144 + token, arr * 72 + row] = 1
                row = (p * 3 + a % 3) * 6 + b % 6
                leave[(80 if a >= 3 else 0) + (40 if b >= 6 else 0) + row, token] = 1
                home = (((a + 3) % 6) * 12 + (b + 6) % 12) * 2 + (p + 1) % 2
                place[(2 if b >= 6 else 0) + (1 if a >= 3 else 0), home, row] = 1
    return [jnp.asarray(m, BF16) for m in (first, second, gather, leave, place)]


def pack_kernel(tok, cot, sel, idx, strip, kept, packed, tok_in, cot_in, sel_in, idx_in, rows, sems):
    copies = [
        pltpu.make_async_copy(src, dst, sems.at[k])
        for k, (src, dst) in enumerate(
            ((tok, tok_in), (cot, cot_in), (sel, sel_in), (idx, idx_in))
        )
    ]
    for copy in copies:
        copy.start()
    for arr, ref in enumerate((tok_in, cot_in)):
        copies[arr].wait()
        for k in range(72):
            at = arr * T + 2 * k
            rows[at : at + 2, :] = ref[k // 12, k % 12].astype(F32)
    copies[2].wait()
    out = dot(sel_in[...], rows[...].astype(BF16)).astype(BF16)
    strip[...] = out[0:T]
    kept[...] = out[T:]
    copies[3].wait()
    packed[0:T, :] = idx_in[:, 0:128]
    packed[T:PACK, :] = packed_rows(idx_in)


def repack_kernel(kept, arrived, sel, strip):
    strip[...] = (dot(sel[0], kept[...]) + dot(sel[1], arrived[...])).astype(BF16)


def unpack_kernel(kept, first, second, sel, out, rows):
    total = dot(sel[0], kept[0]) + dot(sel[1], first[0])
    rows[...] = total + dot(sel[2], second[0]) + dot(sel[3], second[1])
    for k in range(72):
        out[k // 12, k % 12] = rows[2 * k : 2 * k + 2, :].astype(BF16)


def mix_kernel(parts, scattered, out, wide):
    n, rows, _ = out.shape
    bias_rows = scattered.shape[0] // n
    rows = rows - bias_rows
    wide[...] = jnp.sum(parts[...].astype(F32), axis=0)
    for k in range(n):
        mine = wide[rows * k : rows * k + rows, :]
        theirs = scattered[bias_rows * k : bias_rows * k + bias_rows, :]
        out[k] = jnp.concatenate((mine, theirs), axis=0).astype(BF16)


def sum_kernel(parts, out):
    total = jnp.sum(parts[...].astype(F32), axis=0).astype(BF16)
    for k in range(out.shape[0]):
        out[k] = total


def split_kernel(parts, out, scattered, wide):
    n = parts.shape[0]
    bias_rows = scattered.shape[0] // n
    rows = parts.shape[1] - bias_rows
    for k in range(n):
        part = parts[k].astype(F32)
        wide[rows * k : rows * k + rows, :] = part[0:rows]
        scattered[bias_rows * k : bias_rows * k + bias_rows, :] = part[rows:]
    total = wide[...].astype(BF16)
    for k in range(out.shape[0]):
        out[k] = total


def finish_kernel(parts, qkv, proj):
    wide = parts[...].reshape(6 * C, 128).astype(F32)
    for k in range(4):
        qkv[:, 128 * k : 128 * k + 128] = wide[C * k : C * k + C]
    qkv[:, 512:576] = wide[4 * C : 5 * C, 0:64]
    proj[:, 0:64] = wide[4 * C : 5 * C, 64:128]
    proj[:, 64:C] = wide[5 * C : 6 * C]


def packed_rows(idx):
    lane = lax.broadcasted_iota(jnp.int32, (24, 128), 1)
    tail = jnp.zeros((24, 128), jnp.int32)
    for c in range(6):
        part = jnp.concatenate(
            (idx[24 * c : 24 * c + 24, 128:T], jnp.zeros((24, 112), jnp.int32)), axis=1
        )
        part = pltpu.roll(part, 16 * c, 1) if c else part
        tail = jnp.where((lane >= 16 * c) & (lane < 16 * c + 16), part, tail)
    return tail


def bias_body(first, table, col, row, packed, bias, flat):
    def block(i, carry):
        at = pl.ds(pl.multiple_of(i * 8, 8), 8)
        position = packed[at, :]
        low = position & 127
        high = position >> 7
        totals = [jnp.zeros((8, 128), F32)] * HALF
        for k in range(BLKS):
            here = high == k
            for h in range(HALF):
                r = (first + h) * BLKS + k
                values = jnp.broadcast_to(table[r : r + 1, :], (8, 128))
                found = jnp.take_along_axis(values, low, axis=1, mode="promise_in_bounds")
                totals[h] = jnp.where(here, found, totals[h])
        for h in range(HALF):
            flat[h, at, :] = totals[h]
        return carry

    lax.fori_loop(0, PACK // 8, block, 0, unroll=7)
    same = col[...] == row[...]
    for h in range(HALF):
        bias[h, :, 0:128] = jnp.where(same[:, 0:128], flat[h, 0:T, :], -1e9)
        tail = flat[h, T:PACK, :]
        for c in range(6):
            part = pltpu.roll(tail, 128 - 16 * c, 1) if c else tail
            at = slice(24 * c, 24 * c + 24)
            bias[h, at, 128:T] = jnp.where(same[at, 128:T], part[:, 0:16], -1e9)


def bias_first_kernel(packed, table, col, row, bias, flat):
    bias_body(0, table, col, row, packed, bias, flat)


def bias_second_kernel(packed, table, col, row, bias, flat):
    bias_body(HALF, table, col, row, packed, bias, flat)


def main_kernel(kept, lon, lat, sel, bias_a, bias_b, wqkv, wproj,
                grads, ds_out, grad_in_out, normed_out, inv_std_out, cot_out, ds_tail):
    scale = HD ** (-0.5)
    both = dot(sel[0], kept[...]) + dot(sel[1], lon[...]) + dot(sel[2], lat[...])
    values = both[0:T]
    cot = both[T:].astype(BF16)
    center = values - jnp.mean(values, axis=-1, keepdims=True)
    inv_std = lax.rsqrt(jnp.mean(center * center, axis=-1, keepdims=True) + 1e-05)
    normed = center * inv_std
    hidden = normed.astype(BF16)
    proj = dot(hidden, wqkv[...])
    query = proj[:, 0:C]
    query_t = query.T.astype(BF16)
    query = query.astype(BF16)
    key = proj[:, C : 2 * C].astype(BF16)
    value = proj[:, 2 * C :].astype(BF16)
    att = dot(cot, wproj[...], 1, 1)
    att_t = att.T.astype(BF16)
    att = att.astype(BF16)
    head = lax.broadcasted_iota(jnp.int32, (T, C), 1) // HD
    zero = jnp.zeros((T, C), BF16)
    attended = jnp.zeros((T, C), F32)
    grad_query = jnp.zeros((T, C), F32)
    key_t = []
    value_t = []
    lane = lax.broadcasted_iota(jnp.int32, (24, 128), 1)
    masks = [head == h for h in range(HEADS)]
    scores = [dot(jnp.where(m, query, zero), key, 1, 1) * scale for m in masks]
    grad_probs = [dot(jnp.where(m, att, zero), value, 1, 1) for m in masks]
    probs = []
    for h in range(HEADS):
        score = scores[h] + (bias_a[h] if h < HALF else bias_b[h - HALF])
        exponent = jnp.exp(score - jnp.max(score, axis=-1, keepdims=True))
        probs.append(exponent * (1.0 / jnp.sum(exponent, axis=-1, keepdims=True)))
    for h in range(HEADS):
        prob_half = probs[h].astype(BF16)
        attended = attended + dot(prob_half, jnp.where(masks[h], value, zero))
        value_t.append(dot(att_t[HD * h : HD * h + HD], prob_half))
    for h in range(HEADS):
        prob, grad_prob = probs[h], grad_probs[h]
        ds = prob * (grad_prob - jnp.sum(grad_prob * prob, axis=-1, keepdims=True))
        ds_half = ds.astype(BF16)
        grad_query = grad_query + dot(ds_half, jnp.where(masks[h], key, zero))
        key_t.append(dot(query_t[HD * h : HD * h + HD], ds_half))
        ds_out[h, 0:T, :] = ds[:, 0:128]
        ds_tail[:, 0:16] = ds[:, 128:T]
        packed = jnp.zeros((24, 128), F32)
        for c in range(6):
            part = ds_tail[24 * c : 24 * c + 24, :]
            part = pltpu.roll(part, 16 * c, 1) if c else part
            packed = jnp.where((lane >= 16 * c) & (lane < 16 * c + 16), part, packed)
        ds_out[h, T:PACK, :] = packed
    grad_key = jnp.concatenate(key_t, axis=0).T
    grad_value = jnp.concatenate(value_t, axis=0).T
    grad_in = jnp.concatenate((grad_query * scale, grad_key * scale, grad_value), axis=1)
    grad_in = grad_in.astype(BF16)
    grad_qkv = dot(hidden, grad_in, 0, 0)
    grad_proj = dot(attended.astype(BF16), cot, 0, 0)
    both = jnp.concatenate((grad_qkv, grad_proj), axis=1).astype(BF16)
    for k in range(6):
        grads[C * k : C * k + C, :] = both[:, 128 * k : 128 * k + 128]
    grad_in_out[...] = grad_in
    normed_out[...] = normed
    inv_std_out[...] = inv_std
    cot_out[...] = cot


def norm_kernel(grad_in, normed_ref, inv_std, cot, wqkv, leave, ret_kept, ret_strip):
    normed = normed_ref[...]
    grad_hidden = dot(grad_in[...], wqkv[...], 1, 1)
    grad_norm = inv_std[...] * (
        grad_hidden
        - jnp.mean(grad_hidden, axis=-1, keepdims=True)
        - normed * jnp.mean(grad_hidden * normed, axis=-1, keepdims=True)
    )
    returned = (cot[...].astype(F32) + grad_norm).astype(BF16)
    parts = dot(leave[...], returned).astype(BF16)
    for k in range(2):
        ret_kept[k] = parts[40 * k : 40 * k + 40]
        ret_strip[k] = parts[80 + 40 * k : 120 + 40 * k]


def scatter_kernel(packed, ds, out, total):
    total[...] = jnp.zeros_like(total)
    blocks = lax.broadcasted_iota(jnp.int32, (32, 128), 0).astype(F32).astype(BF16)
    lows = lax.broadcasted_iota(jnp.int32, (128, 128), 0).astype(F32).astype(BF16)
    one = jnp.ones((128, 128), BF16)
    none = jnp.zeros((128, 128), BF16)

    def block(i, carry):
        at = pl.ds(pl.multiple_of(i * 8, 8), 8)
        position = packed[at, :]
        low = (position & 127).astype(F32)
        high = (position >> 7).astype(F32)
        left = []
        right = []
        for r in range(8):
            low_row = jnp.broadcast_to(low[r : r + 1], (16, 128)).astype(BF16)
            high_row = jnp.broadcast_to(high[r : r + 1], (16, 128)).astype(BF16)
            right.append(
                jnp.concatenate(
                    [
                        jnp.where(lows[16 * k : 16 * k + 16] == low_row, one[0:16], none[0:16])
                        for k in range(8)
                    ],
                    axis=0,
                )
            )
            mine = [blocks[16 * k : 16 * k + 16] == high_row for k in range(2)]
            parts = []
            for h in range(HEADS):
                row = jnp.broadcast_to(ds[h, at, :][r : r + 1], (16, 128)).astype(BF16)
                parts += [jnp.where(m, row, none[0:16]) for m in mine]
            left.append(jnp.concatenate(parts, axis=0))
        total[...] += dot(jnp.concatenate(left, axis=1), jnp.concatenate(right, axis=1), 1, 1)
        return carry

    lax.fori_loop(0, PACK // 8, block, 0, unroll=7)
    out[...] = total[...]


def call(kernel, shapes, scratch, cost, *args, copies=0):
    scratch = [pltpu.VMEM(s, d) for s, d in scratch]
    specs = {}
    if copies:
        scratch.append(pltpu.SemaphoreType.DMA((copies,)))
        specs["in_specs"] = [pl.BlockSpec(memory_space=pltpu.MemorySpace.HBM)] * copies
    if copies:
        args = [pltpu.with_memory_space_constraint(a, pltpu.MemorySpace.HBM) for a in args]
    return pl.pallas_call(
        kernel,
        out_shape=[jax.ShapeDtypeStruct(s, d) for s, d in shapes],
        scratch_shapes=scratch,
        compiler_params=pltpu.CompilerParams(vmem_limit_bytes=(48 if copies else 48) << 20),
        cost_estimate=pl.CostEstimate(flops=cost, bytes_accessed=1 << 20, transcendentals=0),
        **specs,
    )(*args)


def exchange(block, axes, groups=None):
    return lax.all_to_all(block, axes, 0, 0, axis_index_groups=groups, tiled=False)


def local(sizes, tokens, cotangent, region, pos_index, w_qkv, w_proj, bias_table):
    n_lon, n_lat, n_y = sizes
    n_z = n_lon // n_y
    first, second, gather, leave, place = selections()
    across = ("lat", "rep")

    def moved(block, axes, n, distance):
        return lax.ppermute(block, axes, [((i + distance) % n, i) for i in range(n)])

    table = jnp.pad(bias_table.reshape(ROWS, HEADS).T, ((0, 0), (0, BLKS * 128 - ROWS)))
    table = table.reshape(HEADS * BLKS, 128)

    col, row = region.reshape(T, 1), region.reshape(1, T)
    bias_shape = ((HALF, T, T), F32)
    bias_scratch = [((HALF, PACK, 128), F32)]
    block = ((T, C), BF16)
    order = (1, 2, 0, 3)
    stored = ((6, 12, 2, C), BF16)
    strip, kept, packed = call(
        pack_kernel,
        [block] * 2 + [((PACK, 128), jnp.int32)],
        [stored, stored, ((2 * T, 2 * T), BF16), ((T, T), jnp.int32), ((2 * T, C), F32)],
        10**8,
        tokens.transpose(order), cotangent.transpose(order), first, pos_index,
        copies=4,
    )
    lon = moved(strip, "lon", n_lon, 1)
    (bias_a,) = call(
        bias_first_kernel, [bias_shape], bias_scratch, 3 * 10**9, packed, table, col, row
    )
    (strip,) = call(repack_kernel, [block], [], 10**8, kept, lon, second)
    strip, late_packed = lax.optimization_barrier((strip, packed))
    lat = moved(strip, across, n_lat, 1)
    (bias_b,) = call(
        bias_second_kernel, [bias_shape], bias_scratch, 3 * 10**9, late_packed, table, col, row
    )
    grads, ds, grad_in, normed, inv_std, cot = call(
        main_kernel,
        [
            ((6 * C, 128), BF16),
            ((HEADS, PACK, 128), F32),
            ((T, 3 * C), BF16),
            ((T, C), F32),
            ((T, 1), F32),
            block,
        ],
        [((T, 128), F32)],
        10**10,
        kept, lon, lat, gather, bias_a, bias_b, w_qkv, w_proj,
    )
    rows_y = [[z * n_y + y for y in range(n_y)] for z in range(n_z)]
    rows_z = [[z * n_y + y for z in range(n_z)] for y in range(n_y)]
    rows = 6 * C // n_lat
    grads = exchange(grads.reshape(n_lat, rows, 128), across)
    (scattered,) = call(
        scatter_kernel, [((192, 128), F32)], [((192, 128), F32)], 5 * 10**9, packed, ds
    )
    quarter = ((2, 40, C), BF16)
    ret_kept, ret_strip = call(
        norm_kernel, [quarter] * 2, [], 10**8, grad_in, normed, inv_std, cot, w_qkv, leave
    )
    mixed_rows = (rows + 192) // n_y
    wide = [((rows, 128), F32)]
    (mixed,) = call(
        mix_kernel, [((n_y, mixed_rows, 128), BF16)], wide, 10**7, grads, scattered
    )
    mixed, ret_strip = lax.optimization_barrier((mixed, ret_strip))
    ret_first = moved(ret_strip, across, n_lat, -1)
    mixed = exchange(mixed, "lon", rows_y)
    (mixed,) = call(sum_kernel, [((n_z, mixed_rows, 128), BF16)], [], 10**7, mixed)
    mixed = exchange(mixed, "lon", rows_z)
    (mixed,) = call(sum_kernel, [((n_y, mixed_rows, 128), BF16)], [], 10**7, mixed)
    mixed, ret_first = lax.optimization_barrier((mixed, ret_first))
    ret_second = moved(jnp.stack((ret_kept[1], ret_first[1])), "lon", n_lon, -1)
    mixed = exchange(mixed, "lon", rows_y)
    grads, scattered = call(
        split_kernel, [((n_lat, rows, 128), BF16), ((192, 128), F32)], wide, 10**7, mixed
    )
    grads, ret_second = lax.optimization_barrier((grads, ret_second))
    grads = exchange(grads, across)
    (grad_tokens,) = call(
        unpack_kernel, [((6, 12, 2, C), BF16)], [((T, C), F32)], 10**8,
        ret_kept, ret_first, ret_second, place,
    )
    scattered = scattered.reshape(HEADS, 32 * 128)
    grad_bias = scattered[:, :ROWS].T.reshape(ROWS, 1, HEADS)
    grad_qkv, grad_proj = call(
        finish_kernel, [((C, 3 * C), F32), ((C, C), F32)], [], 10**7, grads
    )
    return (grad_tokens.transpose(2, 0, 1, 3), grad_qkv, grad_proj, grad_bias)


def solution(mesh):
    n_lon = mesh.shape["lon"]
    n_lat = mesh.shape["lat"] * mesh.shape["rep"]
    n_y = 8 if n_lon % 8 == 0 else 2
    placed = (
        P(None, ("lat", "rep"), "lon", None),
        P(None, ("lat", "rep"), "lon", None),
        P(None, ("lat", "rep"), "lon"),
        P(),
        P(),
        P(),
        P(None, ("lat", "rep"), None),
    )
    return jax.shard_map(
        functools.partial(local, (n_lon, n_lat, n_y)),
        mesh=mesh,
        in_specs=placed,
        out_specs=(P(None, ("lat", "rep"), "lon", None), P(), P(), P(None, ("lat", "rep"), None)),
        check_vma=False,
    )
```
